32 devices in a mesh: tm: 8 (over z, x), det: 4 (over y, core).
Axes of the slice: x: 2, y: 2, z: 4, core: 2. Of those that a mesh axis runs over, the one named last changes fastest.
Arguments:
- timestream: float32 [8, 128, 256], P('tm', 'det'), may hold values from -101 to 101
- tile_index: int32 [8, 128, 256], P('tm', 'det'), may hold values from 0 to 31, as said below
- pixel_index: int32 [8, 128, 256], P('tm', 'det'), may hold values from 0 to 32639
- angle_bin: int32 [8, 128, 256], P('tm', 'det'), may hold values from 0 to 1023
- owner_map: int32 [32], replicated, may hold values from 0 to 31, each once
Outputs:
- sky_map: float32 [3, 1044480], P(None, ('tm', 'det'))
- residual: float32 [8, 128, 256], P('tm', 'det')
The draws below stay inside these ranges and needn't reach their ends.
Inputs may be any that keep to these rules, and one draw needn't show every extreme that they name: `tile_index`: among the samples of one device, no tile occurs more than 512 times.
All inputs are finite; a program needn't handle non-finite values.
Results may differ from the reference program's by a relative error of at most 0.00013.
Values sent between devices are 32-bit elements; how exact they have to be, the bound alone decides.
No kernel may reach another device: no remote copies, remote signals or barrier semaphores. Data moves between devices by JAX's collectives and lax.ppermute only.
A program may use at most 320 MiB of HBM per device.

```python
import math
import jax
import jax.numpy as jnp
from jax import lax

MODES = 16
NBINS = 1024
TILE_PIX = 32640
DET_DEV = 32
SAMP_DEV = 256
NBLK = 8
DETS = 128
NTILES = 32
BAND = 16
CAP = 512
NPIX = 1044480


def draw_tile_index(key, part):
    devices = NBLK * (DETS // DET_DEV)
    per_device = DET_DEV * SAMP_DEV
    start_key, order_key = jax.random.split(jax.random.fold_in(key, 11))
    starts = jax.random.randint(start_key, (devices, 1), NTILES - BAND + 1, NTILES + 1)
    orders = jax.vmap(lambda subkey: jax.random.permutation(subkey, per_device))(jax.random.split(order_key, devices))
    tile_ids = (starts + orders // CAP) % NTILES
    return tile_ids.reshape(NBLK, DETS, SAMP_DEV).astype(jnp.int32)


def draw_timestream(key, part):
    subkeys = jax.random.split(jax.random.fold_in(key, 23), 4)
    noise_part = jnp.clip(jax.random.normal(subkeys[0], (NBLK, DETS, SAMP_DEV), jnp.float32), -5.0, 5.0)
    common = 2.0 * jnp.clip(jax.random.normal(subkeys[1], (NBLK, MODES, SAMP_DEV), jnp.float32), -4.0, 4.0)
    det_gain = jnp.exp(jax.random.uniform(subkeys[2], (1, DETS, 1), jnp.float32, math.log(0.5), math.log(2.0)))
    drift_gain = jnp.exp(jax.random.uniform(subkeys[3], (NBLK, DETS, 1), jnp.float32, math.log(0.5), math.log(2.0)))
    amplitude = 1.0 + 2.0 * jnp.arange(NBLK, dtype=jnp.float32).reshape(NBLK, 1, 1) / max(NBLK - 1, 1)
    per_detector = jnp.tile(common, (1, DETS // MODES, 1))
    return (noise_part + amplitude * det_gain * drift_gain * per_detector).astype(jnp.float32)


def touch_ends(drawn, rng, least, high):
    longest = drawn.shape.index(max(drawn.shape))
    spots = []
    for shift in (0, 1):
        where = [jax.random.randint(jax.random.fold_in(rng, axis), (), 0, length) for axis, length in enumerate(drawn.shape)]
        where[longest] = (where[longest] + shift) % drawn.shape[longest]
        spots.append(tuple(where))
    return drawn.at[spots[0]].set(least).at[spots[1]].set(high)


def setup_inputs(seed: int = 0) -> dict:
    keys = jax.random.split(jax.random.key(seed), 6)
    return {
        "timestream": draw_timestream(jax.random.fold_in(keys[5], 71), 0),
        "tile_index": draw_tile_index(jax.random.fold_in(keys[5], 71), 0),
        "pixel_index": touch_ends(jax.random.randint(keys[2], (NBLK, DETS, SAMP_DEV), 0, TILE_PIX), jax.random.fold_in(keys[2], 1), 0, TILE_PIX - 1).astype(jnp.int32),
        "angle_bin": touch_ends(jax.random.randint(keys[3], (NBLK, DETS, SAMP_DEV), 0, NBINS), jax.random.fold_in(keys[3], 1), 0, NBINS - 1).astype(jnp.int32),
        "owner_map": jax.random.permutation(keys[4], NTILES).astype(jnp.int32),
    }


RIDGE = 1.0

def solve_stokes(sums):
    a11 = sums[0] + RIDGE
    a12 = sums[1]
    a13 = sums[2]
    a22 = sums[3] + RIDGE
    a23 = sums[4]
    a33 = sums[5] + RIDGE
    c11 = a22 * a33 - a23 * a23
    c12 = a13 * a23 - a12 * a33
    c13 = a12 * a23 - a13 * a22
    c22 = a11 * a33 - a13 * a13
    c23 = a12 * a13 - a11 * a23
    c33 = a11 * a22 - a12 * a12
    inverse = 1.0 / (a11 * c11 + a12 * c12 + a13 * c13)
    stokes_i = (c11 * sums[6] + c12 * sums[7] + c13 * sums[8]) * inverse
    stokes_q = (c12 * sums[6] + c22 * sums[7] + c23 * sums[8]) * inverse
    stokes_u = (c13 * sums[6] + c23 * sums[7] + c33 * sums[8]) * inverse
    return (stokes_i, stokes_q, stokes_u)

def reference(timestream, tile_index, pixel_index, angle_bin, owner_map):
    blocks, dets, samples = timestream.shape
    grouped = timestream.reshape(blocks, dets // MODES, MODES, samples)
    templates = jnp.sum(grouped, axis=1) / (dets // MODES)
    highest = lax.Precision.HIGHEST
    mode_gram = jnp.einsum('bms,bns->mn', templates, templates, precision=highest)
    mode_proj = jnp.einsum('bds,bms->dm', timestream, templates, precision=highest)
    factor = jnp.linalg.cholesky(mode_gram + RIDGE * jnp.eye(MODES, dtype=mode_gram.dtype))
    mode_coef = jax.scipy.linalg.cho_solve((factor, True), mode_proj.T)
    cleaned = timestream - jnp.einsum('md,bms->bds', mode_coef, templates, precision=highest)
    pol_angle = jnp.pi * angle_bin.astype(jnp.float32) / NBINS
    cosine = jnp.cos(2.0 * pol_angle).reshape(-1)
    sine = jnp.sin(2.0 * pol_angle).reshape(-1)
    values = cleaned.reshape(-1)
    place = (owner_map[tile_index].astype(jnp.int32) * TILE_PIX + pixel_index).reshape(-1).astype(jnp.int32)
    terms = [jnp.ones_like(values), cosine, sine, cosine * cosine, cosine * sine, sine * sine, values, cosine * values, sine * values]
    sums = jnp.stack([jnp.zeros((NPIX,), values.dtype).at[place].add(term) for term in terms])
    stokes_i, stokes_q, stokes_u = solve_stokes(sums)
    predicted = stokes_i[place] + cosine * stokes_q[place] + sine * stokes_u[place]
    residual = (values - predicted).reshape(timestream.shape)
    return (jnp.stack([stokes_i, stokes_q, stokes_u]), residual)
```

```python
import functools

import jax
import jax.numpy as jnp
from jax import lax
from jax.experimental import pallas as pl
from jax.experimental.pallas import tpu as pltpu
from jax.sharding import PartitionSpec as P

MODES = 16
NBINS = 1024
TILE_PIX = 32640
RIDGE = 1.0
LANES = 128
LO = 256
HI = -(-TILE_PIX // LO)
WIN = 32
HIP = HI + WIN - 8
PIX_BITS = 15
HALF = LANES // 2
F32 = jnp.float32
BF16 = jnp.bfloat16
HIGHEST = lax.Precision.HIGHEST
NT = (((1,), (1,)), ((), ()))
NN = (((1,), (0,)), ((), ()))
VMEM_LIMIT = 48 * 1024 * 1024


def iota(shape, dim):
    return lax.broadcasted_iota(jnp.int32, shape, dim)


def split3(x):
    first = x.astype(BF16).astype(F32)
    rest = x - first
    second = rest.astype(BF16).astype(F32)
    return first, second, rest - second


def one_hot_cols(row, rows):
    ids = iota((rows, row.shape[1]), 0).astype(F32).astype(BF16)
    want = jnp.broadcast_to(row.astype(F32).astype(BF16), ids.shape)
    return jnp.where(ids == want, jnp.ones_like(ids), jnp.zeros_like(ids))


def route_kernel(owner_ref, key_ref, load_ref, send_ref, idx_ref, keys, loads):
    tiles, rows = idx_ref.shape[0], idx_ref.shape[1]
    depth = key_ref.shape[0]
    keys[0:depth, :] = key_ref[...]
    loads[0:depth, :] = load_ref[...]
    keys[depth:, :] = jnp.zeros((8, LANES), jnp.int32)
    loads[depth:, :] = jnp.zeros((8, LANES), jnp.int32)
    sorted_keys = key_ref[...]
    lane = iota((8, LANES), 1)
    slot = iota((8, LANES), 0) * LANES + lane
    starts = [jnp.int32(0)]
    for tile in range(1, tiles):
        below = (sorted_keys < (tile << PIX_BITS)).astype(F32)
        starts.append(jnp.sum(below).astype(jnp.int32))
    starts.append(jnp.int32(depth * LANES))
    for tile in range(tiles):
        start = starts[tile]
        count = starts[tile + 1] - start
        top = start // LANES
        shift = start % LANES
        back = lax.rem(LANES - shift, LANES)
        whole = lane < LANES - shift

        def run(ref):
            turned = pltpu.roll(ref[pl.ds(top, 8), :], back, 1)
            return jnp.where(whole, turned, pltpu.roll(turned, 7, 0))

        key = run(keys)
        load = run(loads)
        live = slot < count
        owner = owner_ref[tile]
        pixel = jnp.where(live, key & ((1 << PIX_BITS) - 1), -1)
        index = jnp.where(live, load >> 10, -1)
        send_ref[owner, 0:rows, :] = pixel[0:rows]
        send_ref[owner, rows : 2 * rows, :] = (load & (NBINS - 1))[0:rows]
        idx_ref[owner, :, :] = index[0:rows]


def route(key, load, owner_map, owners, rows):
    flat = key.shape[0]
    depth = flat // LANES
    return pl.pallas_call(
        route_kernel,
        out_shape=(
            jax.ShapeDtypeStruct((owners, 2 * rows, LANES), jnp.int32),
            jax.ShapeDtypeStruct((owners, rows, LANES), jnp.int32),
        ),
        in_specs=[
            pl.BlockSpec(memory_space=pltpu.SMEM),
            pl.BlockSpec(memory_space=pltpu.VMEM),
            pl.BlockSpec(memory_space=pltpu.VMEM),
        ],
        scratch_shapes=[
            pltpu.VMEM((depth + 8, LANES), jnp.int32),
            pltpu.VMEM((depth + 8, LANES), jnp.int32),
        ],
        name="route",
    )(owner_map, key.reshape(depth, LANES), load.reshape(depth, LANES))


def modes_kernel(members, copies, parts_ref, samples_ref, temp_ref, out_ref):
    templates = jnp.sum(parts_ref[...], axis=0) / members
    temp_ref[...] = templates
    both = jnp.concatenate([templates, samples_ref[...]], axis=0)
    products = lax.dot_general(templates, both, NT, precision=HIGHEST, preferred_element_type=F32)
    pad = jnp.zeros((MODES, HALF - products.shape[1]), F32)
    half = jnp.concatenate([products, pad], axis=1)
    packed = jnp.concatenate([half[: MODES // 2], half[MODES // 2 :]], axis=1)
    for i in range(copies):
        out_ref[i] = packed


def modes(parts, samples, members, copies):
    return pl.pallas_call(
        functools.partial(modes_kernel, members, copies),
        out_shape=(
            jax.ShapeDtypeStruct((MODES, samples.shape[1]), F32),
            jax.ShapeDtypeStruct((copies, MODES // 2, LANES), F32),
        ),
        name="modes",
    )(parts, samples)


def clean_kernel(sums_ref, temp_ref, samples_ref, idx_ref, clean_ref, pay_ref):
    det_local, length = samples_ref.shape
    owners, rows = idx_ref.shape[0], idx_ref.shape[1]
    packed = jnp.sum(sums_ref[...], axis=0)
    system = jnp.concatenate([packed, pltpu.roll(packed, HALF, 1)], axis=0)
    row_id = iota((MODES, LANES), 0)
    lane_id = iota((MODES, LANES), 1)
    system = system + jnp.where(row_id == lane_id, RIDGE, 0.0)
    for k in range(MODES):
        pivot = system[k : k + 1, :] / system[k : k + 1, k : k + 1]
        column = system[:, k : k + 1]
        system = jnp.where(row_id == k, pivot, system - column * pivot)
    coef = system[:, MODES : MODES + det_local]
    model = lax.dot_general(
        coef, temp_ref[...], (((0,), (0,)), ((), ())), precision=HIGHEST, preferred_element_type=F32
    )
    cleaned = samples_ref[...] - model
    clean_ref[...] = cleaned
    parts = jnp.concatenate([x.astype(BF16) for x in split3(cleaned)], axis=0)
    det_id = iota((det_local, 2 * LANES), 0)

    def step(pair, _):
        for r in range(rows):
            index = jnp.concatenate(
                [idx_ref[2 * pair, r : r + 1, :], idx_ref[2 * pair + 1, r : r + 1, :]], axis=1
            )
            picked = lax.dot_general(
                parts, one_hot_cols(index & (length - 1), length), NN, preferred_element_type=F32
            )
            total = picked[:det_local] + picked[det_local : 2 * det_local] + picked[2 * det_local :]
            here = jnp.where(det_id == index // length, total, 0.0)
            value = jnp.sum(here, axis=0, keepdims=True)
            pay_ref[2 * pair, r : r + 1, :] = value[:, :LANES]
            pay_ref[2 * pair + 1, r : r + 1, :] = value[:, LANES:]
        return 0

    lax.fori_loop(0, owners // 2, step, 0, unroll=2)


def clean(sums, templates, samples, idx):
    return pl.pallas_call(
        clean_kernel,
        out_shape=(
            jax.ShapeDtypeStruct(samples.shape, F32),
            jax.ShapeDtypeStruct(idx.shape, F32),
        ),
        name="clean",
    )(sums, templates, samples, idx)


def shuffle(first, second, lane):
    return (
        jnp.where(lane < HALF, first, pltpu.roll(second, HALF, 1)),
        jnp.where(lane < HALF, pltpu.roll(first, HALF, 1), second),
    )


def chunk_row(ref, half, quad, r):
    return jnp.concatenate(
        [ref[half, 2 * quad, pl.ds(r, 1), :], ref[half, 2 * quad + 1, pl.ds(r, 1), :]], axis=1
    )


def window(table_ref, half, quad, r):
    at = 2 * (2 * quad + half)
    return table_ref[r, at], table_ref[r, at + 1]


def scatter_add(acc_ref, first, row_hi, one_lo, terms):
    start = pl.multiple_of(first * 8, 8)
    here = (iota((WIN, row_hi.shape[1]), 0) + start) == row_hi
    stacked = [
        jnp.where(here, jnp.broadcast_to(piece, here.shape), 0.0).astype(BF16)
        for pieces in terms
        for piece in pieces
    ]
    found = lax.dot_general(
        jnp.concatenate(stacked, axis=0), one_lo, NT, preferred_element_type=F32
    )
    at = 0
    for q, pieces in enumerate(terms):
        total = found[at : at + WIN]
        at += WIN
        for _ in pieces[1:]:
            total = total + found[at : at + WIN]
            at += WIN
        acc_ref[q, pl.ds(start, WIN), :] += total


def over_chunks(quads, rows, table_ref, body):
    def step(quad, _):
        def live(r, half):
            lowest, highest = window(table_ref, half, quad, r)
            return highest - lowest

        spans = [live(r, half) for r in range(rows) for half in range(2)]
        widest = functools.reduce(jnp.maximum, spans)

        @pl.when(widest >= 0)
        def _():
            for r in range(rows):
                for half in range(2):
                    body(half, quad, r, window(table_ref, half, quad, r)[0], True)

        @pl.when(widest >= WIN // 8)
        def _():
            def chunk(i, _):
                r, half = i // 2, i % 2
                lowest, highest = window(table_ref, half, quad, r)

                def more(w, _):
                    body(half, quad, r, lowest + w * (WIN // 8), False)
                    return 0

                lax.fori_loop(1, (highest - lowest) // (WIN // 8) + 1, more, 0)
                return 0

            lax.fori_loop(0, 2 * rows, chunk, 0)

        return 0

    lax.fori_loop(0, quads, step, 0)


def angles_kernel(got_ref, acc_ref, pix_ref, cos_ref, sin_ref, table_ref, table_vmem, table, sem):
    owners, rows = got_ref.shape[0], got_ref.shape[1] // 2
    lane = iota((2 * rows, LANES), 1)
    table_lane = iota((rows, LANES), 1)
    windows = jnp.zeros((rows, LANES), jnp.int32)
    for quad in range(owners // 4):
        ends = [[], []]
        for sub in range(2):
            pair = 2 * quad + sub
            mixed = shuffle(got_ref[2 * pair], got_ref[2 * pair + 1], lane)
            for half in range(2):
                pixel = mixed[half][:rows]
                pix_ref[half, pair] = pixel
                angle = (jnp.pi * mixed[half][rows:].astype(F32) / NBINS) * 2.0
                cos_ref[half, pair] = jnp.cos(angle)
                sin_ref[half, pair] = jnp.sin(angle)
                ends[half].append(pixel)
        for half in range(2):
            a, b = ends[half]
            most = jnp.maximum(a, b)
            least = jnp.minimum(
                jnp.where(a < 0, TILE_PIX - 1, a), jnp.where(b < 0, TILE_PIX - 1, b)
            )
            most = jnp.max(most, axis=1, keepdims=True)
            least = jnp.min(least, axis=1, keepdims=True)
            high = most >> 11
            low = jnp.where(most < 0, 0, least >> 11)
            at = 2 * (2 * quad + half)
            windows = jnp.where(table_lane == at, low, windows)
            windows = jnp.where(table_lane == at + 1, high, windows)
    table_vmem[...] = windows
    table_ref[...] = windows
    copy = pltpu.make_async_copy(table_vmem, table, sem)
    copy.start()
    acc_ref[...] = jnp.zeros_like(acc_ref)
    copy.wait()

    def body(half, quad, r, first, _):
        pixel = chunk_row(pix_ref, half, quad, r)
        one_lo = one_hot_cols(pixel & (LO - 1), LO)
        cosine = chunk_row(cos_ref, half, quad, r)
        sine = chunk_row(sin_ref, half, quad, r)
        terms = [
            (jnp.ones_like(cosine),),
            split3(cosine),
            split3(sine),
            split3(cosine * cosine),
            split3(cosine * sine),
            split3(sine * sine),
        ]
        scatter_add(acc_ref, first, pixel >> 8, one_lo, terms)

    over_chunks(owners // 4, rows, table, body)


def angles(got):
    owners, rows = got.shape[0], got.shape[1] // 2
    mixed = (2, owners // 2, rows, LANES)
    return pl.pallas_call(
        angles_kernel,
        out_shape=(
            jax.ShapeDtypeStruct((6, HIP, LO), F32),
            jax.ShapeDtypeStruct(mixed, jnp.int32),
            jax.ShapeDtypeStruct(mixed, F32),
            jax.ShapeDtypeStruct(mixed, F32),
            jax.ShapeDtypeStruct((rows, LANES), jnp.int32),
        ),
        scratch_shapes=[
            pltpu.VMEM((rows, LANES), jnp.int32),
            pltpu.SMEM((rows, LANES), jnp.int32),
            pltpu.SemaphoreType.DMA,
        ],
        compiler_params=pltpu.CompilerParams(vmem_limit_bytes=VMEM_LIMIT),
        name="angles",
    )(got)


def solve_stokes(sums):
    a11 = sums[0] + RIDGE
    a12 = sums[1]
    a13 = sums[2]
    a22 = sums[3] + RIDGE
    a23 = sums[4]
    a33 = sums[5] + RIDGE
    c11 = a22 * a33 - a23 * a23
    c12 = a13 * a23 - a12 * a33
    c13 = a12 * a23 - a13 * a22
    c22 = a11 * a33 - a13 * a13
    c23 = a12 * a13 - a11 * a23
    c33 = a11 * a22 - a12 * a12
    inverse = 1.0 / (a11 * c11 + a12 * c12 + a13 * c13)
    stokes_i = (c11 * sums[6] + c12 * sums[7] + c13 * sums[8]) * inverse
    stokes_q = (c12 * sums[6] + c22 * sums[7] + c23 * sums[8]) * inverse
    stokes_u = (c13 * sums[6] + c23 * sums[7] + c33 * sums[8]) * inverse
    return (stokes_i, stokes_q, stokes_u)


def map_kernel(
    table, got_ref, acc_ref, pix_ref, cos_ref, sin_ref, sky_ref, back_ref, value_ref, rhs_ref
):
    owners, rows = got_ref.shape[0], got_ref.shape[1]
    lane = iota((rows, LANES), 1)
    for pair in range(owners // 2):
        mixed = shuffle(got_ref[2 * pair], got_ref[2 * pair + 1], lane)
        for half in range(2):
            value_ref[half, pair] = mixed[half]
    rhs_ref[...] = jnp.zeros_like(rhs_ref)

    def add(half, quad, r, first, _):
        pixel = chunk_row(pix_ref, half, quad, r)
        one_lo = one_hot_cols(pixel & (LO - 1), LO)
        value = chunk_row(value_ref, half, quad, r)
        terms = [
            split3(value),
            split3(chunk_row(cos_ref, half, quad, r) * value),
            split3(chunk_row(sin_ref, half, quad, r) * value),
        ]
        scatter_add(rhs_ref, first, pixel >> 8, one_lo, terms)

    over_chunks(owners // 4, rows, table, add)

    for block in range(HI // 8):
        at = pl.ds(block * 8, 8)
        stokes = solve_stokes([acc_ref[q, at, :] for q in range(6)] + [rhs_ref[q, at, :] for q in range(3)])
        for q in range(3):
            rhs_ref[q, at, :] = stokes[q]
            for i in range(8):
                first = (block * 8 + i) * LO
                width = min(LO, TILE_PIX - first)
                sky_ref[q : q + 1, first : first + width] = stokes[q][i : i + 1, :width]

    value_ref[...] = jnp.zeros_like(value_ref)

    def look(half, quad, r, first, fresh):
        pixel = chunk_row(pix_ref, half, quad, r)
        one_lo = one_hot_cols(pixel & (LO - 1), LO)
        start = pl.multiple_of(first * 8, 8)
        planes = [split3(rhs_ref[q, pl.ds(start, WIN), :]) for q in range(3)]
        found = lax.dot_general(
            jnp.concatenate([x.astype(BF16) for plane in planes for x in plane], axis=0),
            one_lo,
            NN,
            preferred_element_type=F32,
        )
        stokes = [
            found[3 * q * WIN : (3 * q + 1) * WIN]
            + found[(3 * q + 1) * WIN : (3 * q + 2) * WIN]
            + found[(3 * q + 2) * WIN : (3 * q + 3) * WIN]
            for q in range(3)
        ]
        cosine = chunk_row(cos_ref, half, quad, r)
        sine = chunk_row(sin_ref, half, quad, r)
        signal = stokes[0] + cosine * stokes[1] + sine * stokes[2]
        here = (iota(signal.shape, 0) + start) == (pixel >> 8)
        value = jnp.sum(jnp.where(here, signal, 0.0), axis=0, keepdims=True)
        for sub in range(2):
            part = value[:, sub * LANES : (sub + 1) * LANES]
            if fresh:
                value_ref[half, 2 * quad + sub, pl.ds(r, 1), :] = part
            else:
                value_ref[half, 2 * quad + sub, pl.ds(r, 1), :] += part

    over_chunks(owners // 4, rows, table, look)

    for pair in range(owners // 2):
        low, high = value_ref[0, pair], value_ref[1, pair]
        back_ref[2 * pair] = jnp.where(lane < HALF, low, pltpu.roll(high, HALF, 1))
        back_ref[2 * pair + 1] = jnp.where(lane < HALF, pltpu.roll(low, HALF, 1), high)


def make_map(table, got, acc, pixels, cosines, sines):
    vmem = pl.BlockSpec(memory_space=pltpu.VMEM)
    return pl.pallas_call(
        map_kernel,
        out_shape=(
            jax.ShapeDtypeStruct((3, TILE_PIX), F32),
            jax.ShapeDtypeStruct(got.shape, F32),
        ),
        in_specs=[pl.BlockSpec(memory_space=pltpu.SMEM)] + [vmem] * 5,
        scratch_shapes=[pltpu.VMEM(pixels.shape, F32), pltpu.VMEM((3, HIP, LO), F32)],
        compiler_params=pltpu.CompilerParams(vmem_limit_bytes=VMEM_LIMIT),
        name="make_map",
    )(table, got, acc, pixels, cosines, sines)


def residual_kernel(got_ref, idx_ref, clean_ref, out_ref):
    det_local, length = clean_ref.shape
    owners, rows = idx_ref.shape[0], idx_ref.shape[1]
    det_id = iota((det_local, 2 * LANES), 0)

    def step(pair, total):
        for r in range(rows):
            index = jnp.concatenate(
                [idx_ref[2 * pair, r : r + 1, :], idx_ref[2 * pair + 1, r : r + 1, :]], axis=1
            )
            value = jnp.concatenate(
                [got_ref[2 * pair, r : r + 1, :], got_ref[2 * pair + 1, r : r + 1, :]], axis=1
            )
            here = det_id == index // length
            stacked = [
                jnp.where(here, jnp.broadcast_to(piece, here.shape), 0.0).astype(BF16)
                for piece in split3(value)
            ]
            total = total + lax.dot_general(
                jnp.concatenate(stacked, axis=0),
                one_hot_cols(index & (length - 1), length),
                NT,
                preferred_element_type=F32,
            )
        return total

    total = lax.fori_loop(
        0, owners // 2, step, jnp.zeros((3 * det_local, length), F32), unroll=2
    )
    signal = total[:det_local] + total[det_local : 2 * det_local] + total[2 * det_local :]
    out_ref[...] = clean_ref[...] - signal


def residuals(got, idx, cleaned):
    return pl.pallas_call(
        residual_kernel, out_shape=jax.ShapeDtypeStruct(cleaned.shape, F32), name="residuals"
    )(got, idx, cleaned)


def shards(timestream, tile_index, pixel_index, angle_bin, owner_map):
    blocks, det_local, sample_local = timestream.shape
    samples = timestream[0]
    tm_count = lax.axis_size("tm")
    det_count = lax.axis_size("det")
    owners = tm_count * det_count
    flat = det_local * sample_local
    rows = flat // (owners // 2) // LANES

    partial = jnp.sum(samples.reshape(det_local // MODES, MODES, sample_local), axis=0)
    partials = lax.all_gather(partial, "det")
    templates, products = modes(partials, samples, det_local * det_count // MODES, tm_count)
    products = lax.all_to_all(products, "tm", split_axis=0, concat_axis=0, tiled=True)

    key = (tile_index.reshape(-1) << PIX_BITS) + pixel_index.reshape(-1)
    load = (jnp.arange(flat, dtype=jnp.int32) << 10) + angle_bin.reshape(-1)
    key, load = lax.sort((key, load), num_keys=1, is_stable=False)
    send, idx = route(key, load, owner_map, owners, rows)
    everywhere = functools.partial(
        lax.all_to_all, axis_name=("tm", "det"), split_axis=0, concat_axis=0, tiled=True
    )
    got = everywhere(send)
    acc, pixels, cosines, sines, table = angles(got)

    cleaned, pay = clean(products, templates, samples, idx)
    values = everywhere(pay)
    sky, back = make_map(table, values, acc, pixels, cosines, sines)
    residual = residuals(everywhere(back), idx, cleaned)
    return (sky, residual.reshape(blocks, det_local, sample_local))


def solution(mesh):
    placed = (
        P("tm", "det", None),
        P("tm", "det", None),
        P("tm", "det", None),
        P("tm", "det", None),
        P(),
    )
    return jax.shard_map(
        shards,
        mesh=mesh,
        in_specs=placed,
        out_specs=(P(None, ("tm", "det")), P("tm", "det", None)),
        check_vma=False,
    )
```

```python
import functools

import jax
import jax.numpy as jnp
from jax import lax
from jax.experimental import pallas as pl
from jax.experimental.pallas import tpu as pltpu
from jax.sharding import PartitionSpec as P

MODES = 16
NBINS = 1024
TILE_PIX = 32640
RIDGE = 1.0
LANES = 128
LO = 256
HI = -(-TILE_PIX // LO)
WIN = 32
HIP = HI + WIN - 8
SUB = 32
WAYS = LANES // SUB
GROUP = 8
PIX_BITS = 15
HALF = LANES // 2
F32 = jnp.float32
BF16 = jnp.bfloat16
HIGHEST = lax.Precision.HIGHEST
NT = (((1,), (1,)), ((), ()))
NN = (((1,), (0,)), ((), ()))
VMEM_LIMIT = 24 * 1024 * 1024
VMEM_SPEC = pl.BlockSpec(memory_space=pltpu.VMEM)


def iota(shape, dim):
    return lax.broadcasted_iota(jnp.int32, shape, dim)


def split3(x):
    first = x.astype(BF16).astype(F32)
    rest = x - first
    second = rest.astype(BF16).astype(F32)
    return first, second, rest - second


def split2(x):
    return split3(x)[:2]


def one_hot_cols(row, rows):
    ids = iota((rows, row.shape[1]), 0).astype(F32).astype(BF16)
    want = jnp.broadcast_to(row.astype(F32).astype(BF16), ids.shape)
    return jnp.where(ids == want, jnp.ones_like(ids), jnp.zeros_like(ids))


def modes_kernel(members, copies, *refs):
    part_refs = refs[:-2]
    temp_ref, out_ref = refs[-2:]
    own_ref = part_refs[0]
    groups = own_ref.shape[0] // MODES
    templates = sum(ref[g * MODES : (g + 1) * MODES, :] for ref in part_refs for g in range(groups))
    templates = templates / members
    temp_ref[...] = templates
    both = jnp.concatenate([templates, own_ref[...]], axis=0)
    products = lax.dot_general(templates, both, NT, precision=HIGHEST, preferred_element_type=F32)
    pad = jnp.zeros((MODES, HALF - products.shape[1]), F32)
    half = jnp.concatenate([products, pad], axis=1)
    packed = jnp.concatenate([half[: MODES // 2], half[MODES // 2 :]], axis=1)
    for i in range(copies):
        out_ref[i] = packed


def modes(parts, members, copies):
    return pl.pallas_call(
        functools.partial(modes_kernel, members, copies),
        out_shape=(
            jax.ShapeDtypeStruct((MODES, parts[0].shape[1]), F32),
            jax.ShapeDtypeStruct((copies, MODES // 2, LANES), F32),
        ),
        in_specs=[VMEM_SPEC] * len(parts),
        out_specs=(VMEM_SPEC, VMEM_SPEC),
        compiler_params=pltpu.CompilerParams(vmem_limit_bytes=VMEM_LIMIT),
        name="modes",
    )(*parts)


def route_kernel(owner_ref, key_ref, load_ref, send_ref, idx_ref, keys, loads):
    tiles, rows = idx_ref.shape[0], idx_ref.shape[1]
    depth = key_ref.shape[0]
    keys[0:depth, :] = key_ref[...]
    loads[0:depth, :] = load_ref[...]
    keys[depth:, :] = jnp.zeros((8, LANES), jnp.int32)
    loads[depth:, :] = jnp.zeros((8, LANES), jnp.int32)
    sorted_keys = key_ref[...]
    lane = iota((8, LANES), 1)
    slot = iota((8, LANES), 0) * LANES + lane
    starts = [jnp.int32(0)]
    for tile in range(1, tiles):
        below = (sorted_keys < (tile << PIX_BITS)).astype(F32)
        starts.append(jnp.sum(below).astype(jnp.int32))
    starts.append(jnp.int32(depth * LANES))
    for tile in range(tiles):
        start = starts[tile]
        count = starts[tile + 1] - start
        top = start // LANES
        shift = start % LANES
        back = lax.rem(LANES - shift, LANES)
        whole = lane < LANES - shift

        def run(ref):
            turned = pltpu.roll(ref[pl.ds(top, 8), :], back, 1)
            return jnp.where(whole, turned, pltpu.roll(turned, 7, 0))

        key = run(keys)
        load = run(loads)
        live = slot < count
        owner = owner_ref[tile]
        pixel = jnp.where(live, key & ((1 << PIX_BITS) - 1), -1)
        index = jnp.where(live, load >> 10, -1)
        send_ref[owner, 0:rows, :] = pixel[0:rows]
        send_ref[owner, rows : 2 * rows, :] = (load & (NBINS - 1))[0:rows]
        idx_ref[owner, :, :] = index[0:rows]


def route(key, load, owner_map, owners, rows):
    flat = key.shape[0]
    depth = flat // LANES
    return pl.pallas_call(
        route_kernel,
        out_shape=(
            jax.ShapeDtypeStruct((owners, 2 * rows, LANES), jnp.int32),
            jax.ShapeDtypeStruct((owners, rows, LANES), jnp.int32),
        ),
        in_specs=[pl.BlockSpec(memory_space=pltpu.SMEM), VMEM_SPEC, VMEM_SPEC],
        out_specs=(VMEM_SPEC, VMEM_SPEC),
        scratch_shapes=[
            pltpu.VMEM((depth + 8, LANES), jnp.int32),
            pltpu.VMEM((depth + 8, LANES), jnp.int32),
        ],
        compiler_params=pltpu.CompilerParams(vmem_limit_bytes=VMEM_LIMIT),
        name="route",
    )(owner_map, key.reshape(depth, LANES), load.reshape(depth, LANES))


def clean_kernel(sums_ref, temp_ref, samples_ref, idx_ref, clean_ref, pay_ref):
    det_local, length = samples_ref.shape
    owners, rows = idx_ref.shape[0], idx_ref.shape[1]
    packed = jnp.sum(sums_ref[...], axis=0)
    system = jnp.concatenate([packed, pltpu.roll(packed, HALF, 1)], axis=0)
    row_id = iota((MODES, LANES), 0)
    lane_id = iota((MODES, LANES), 1)
    system = system + jnp.where(row_id == lane_id, RIDGE, 0.0)
    for k in range(MODES):
        pivot = system[k : k + 1, :] / system[k : k + 1, k : k + 1]
        column = system[:, k : k + 1]
        system = jnp.where(row_id == k, pivot, system - column * pivot)
    coef = system[:, MODES : MODES + det_local]
    model = lax.dot_general(
        coef, temp_ref[...], (((0,), (0,)), ((), ())), precision=HIGHEST, preferred_element_type=F32
    )
    cleaned = samples_ref[...] - model
    clean_ref[...] = cleaned
    parts = jnp.concatenate(split2(cleaned), axis=0).astype(BF16)
    det_id = iota((det_local, 2 * LANES), 0)

    def step(pair, _):
        for r in range(rows):
            index = jnp.concatenate(
                [idx_ref[2 * pair, r : r + 1, :], idx_ref[2 * pair + 1, r : r + 1, :]], axis=1
            )
            picked = lax.dot_general(
                parts, one_hot_cols(index & (length - 1), length), NN, preferred_element_type=F32
            )
            total = picked[:det_local] + picked[det_local:]
            here = jnp.where(det_id == index // length, total, 0.0)
            value = jnp.sum(here, axis=0, keepdims=True)
            pay_ref[2 * pair, r : r + 1, :] = value[:, :LANES]
            pay_ref[2 * pair + 1, r : r + 1, :] = value[:, LANES:]
        return 0

    lax.fori_loop(0, owners // 2, step, 0, unroll=4)


def clean(sums, templates, samples, idx):
    return pl.pallas_call(
        clean_kernel,
        out_shape=(
            jax.ShapeDtypeStruct(samples.shape, F32),
            jax.ShapeDtypeStruct(idx.shape, F32),
        ),
        in_specs=[VMEM_SPEC] * 4,
        out_specs=(VMEM_SPEC, VMEM_SPEC),
        compiler_params=pltpu.CompilerParams(vmem_limit_bytes=VMEM_LIMIT),
        name="clean",
    )(sums, templates, samples, idx)


def shuffle(blocks, lane):
    blocks = list(blocks)
    width = HALF
    while width >= SUB:
        low = (lane & width) == 0
        step = width // SUB
        for i in range(WAYS):
            if i & step == 0:
                a, b = blocks[i], blocks[i + step]
                blocks[i] = jnp.where(low, a, pltpu.roll(b, width, 1))
                blocks[i + step] = jnp.where(low, pltpu.roll(a, LANES - width, 1), b)
        width //= 2
    return blocks


def chunk_row(ref, run, group, r):
    return jnp.concatenate([ref[run, GROUP * group + i, r : r + 1, :] for i in range(GROUP)], axis=1)


def over_chunks(groups, rows, table_ref, body):
    def step(i, _):
        run, group = lax.rem(i, WAYS), lax.div(i, WAYS)
        ends = [(table_ref[r, 2 * i], table_ref[r, 2 * i + 1]) for r in range(rows)]
        widest = functools.reduce(jnp.maximum, [high - low for low, high in ends])

        for r in range(rows):
            body(run, group, r, ends[r][0], True)

        @pl.when(widest >= WIN // 8)
        def _():
            for r in range(rows):
                low, high = ends[r]

                def more(w, _):
                    body(run, group, r, low + w * (WIN // 8), False)
                    return 0

                lax.fori_loop(1, (high - low) // (WIN // 8) + 1, more, 0)

        return 0

    lax.fori_loop(0, groups * WAYS, step, 0)


def prepare_kernel(got_ref, mixed_ref):
    owners, rows = got_ref.shape[0], mixed_ref.shape[3]
    lane = iota((2 * rows, LANES), 1)
    for at in range(owners // WAYS):
        mixed = shuffle([got_ref[at * WAYS + i] for i in range(WAYS)], lane)
        for run in range(WAYS):
            mixed_ref[0, run, at] = mixed[run][:rows].astype(F32)
            angle = (jnp.pi * mixed[run][rows:].astype(F32) / NBINS) * 2.0
            mixed_ref[1, run, at] = jnp.cos(angle)
            mixed_ref[2, run, at] = jnp.sin(angle)


def prepare(got, rows):
    return pl.pallas_call(
        prepare_kernel,
        out_shape=jax.ShapeDtypeStruct((3, WAYS, got.shape[0] // WAYS, rows, LANES), F32),
        in_specs=[VMEM_SPEC],
        out_specs=VMEM_SPEC,
        compiler_params=pltpu.CompilerParams(vmem_limit_bytes=VMEM_LIMIT),
        name="prepare",
    )(got)


def windows_of(pix_ref, groups, rows):
    table_lane = iota((rows, LANES), 1)
    windows = jnp.zeros((rows, LANES), jnp.int32)
    for group in range(groups):
        for run in range(WAYS):
            ends = [pix_ref[run, group * GROUP + i] for i in range(GROUP)]
            most = functools.reduce(jnp.maximum, ends)
            least = functools.reduce(
                jnp.minimum, [jnp.where(x < 0, TILE_PIX - 1, x) for x in ends]
            )
            most = jnp.max(most, axis=1, keepdims=True)
            least = jnp.min(least, axis=1, keepdims=True)
            high = most >> 11
            low = jnp.where(most < 0, 0, least >> 11)
            at = 2 * (group * WAYS + run)
            windows = jnp.where(table_lane == at, low, windows)
            windows = jnp.where(table_lane == at + 1, high, windows)
    return windows


PARTS = 20


def solve_stokes(sums):
    a11 = sums[0] + RIDGE
    a12 = sums[1]
    a13 = sums[2]
    a22 = sums[3] + RIDGE
    a23 = sums[4]
    a33 = sums[5] + RIDGE
    c11 = a22 * a33 - a23 * a23
    c12 = a13 * a23 - a12 * a33
    c13 = a12 * a23 - a13 * a22
    c22 = a11 * a33 - a13 * a13
    c23 = a12 * a13 - a11 * a23
    c33 = a11 * a22 - a12 * a12
    inverse = 1.0 / (a11 * c11 + a12 * c12 + a13 * c13)
    stokes_i = (c11 * sums[6] + c12 * sums[7] + c13 * sums[8]) * inverse
    stokes_q = (c12 * sums[6] + c22 * sums[7] + c23 * sums[8]) * inverse
    stokes_u = (c13 * sums[6] + c23 * sums[7] + c33 * sums[8]) * inverse
    return (stokes_i, stokes_q, stokes_u)


def map_kernel(
    got_ref, mixed_ref, sky_ref, back_ref, pix_ref, parts_ref, sum_ref, table_vmem, table, sem
):
    owners, rows = got_ref.shape[0], got_ref.shape[1]
    groups = owners // WAYS // GROUP
    lane = iota((rows, LANES), 1)
    cos_ref, sin_ref = mixed_ref.at[1], mixed_ref.at[2]
    pix_ref[...] = mixed_ref[0].astype(jnp.int32)
    table_vmem[...] = windows_of(pix_ref, groups, rows)
    copy = pltpu.make_async_copy(table_vmem, table, sem)
    copy.start()
    for at in range(owners // WAYS):
        mixed = shuffle([got_ref[at * WAYS + i] for i in range(WAYS)], lane)
        for run in range(WAYS):
            value, cosine, sine = mixed[run], cos_ref[run, at], sin_ref[run, at]
            parts = (
                split3(cosine)
                + split3(sine)
                + split3(cosine * cosine)
                + split3(cosine * sine)
                + split2(value)
                + split3(cosine * value)
                + split3(sine * value)
            )
            for p, part in enumerate(parts):
                parts_ref[p, run, at] = part
    sum_ref[...] = jnp.zeros_like(sum_ref)
    copy.wait()
    terms = (1, 3, 3, 3, 3, 2, 3, 3)

    def add(run, group, r, first, _):
        pixel = chunk_row(pix_ref, run, group, r)
        start = pl.multiple_of(first * 8, 8)
        here = (iota((WIN, pixel.shape[1]), 0) + start) == (pixel >> 8)
        pieces = [jnp.ones(pixel.shape, F32)]
        pieces += [chunk_row(parts_ref.at[p], run, group, r) for p in range(PARTS)]
        stacked = [jnp.where(here, jnp.broadcast_to(x, here.shape), 0.0) for x in pieces]
        found = lax.dot_general(
            jnp.concatenate(stacked, axis=0).astype(BF16),
            one_hot_cols(pixel & (LO - 1), LO),
            NT,
            preferred_element_type=F32,
        )
        at = 0
        for q, count in enumerate(terms):
            total = found[at : at + WIN]
            for i in range(1, count):
                total = total + found[at + i * WIN : at + (i + 1) * WIN]
            at += count * WIN
            sum_ref[q, pl.ds(start, WIN), :] += total

    over_chunks(groups, rows, table, add)

    for block in range(HI // 8):
        at = pl.ds(block * 8, 8)
        sums = [sum_ref[q, at, :] for q in range(8)]
        stokes = solve_stokes(sums[:5] + [sums[0] - sums[3]] + sums[5:])
        for q in range(3):
            sum_ref[q, at, :] = stokes[q]
            for i in range(8):
                first = (block * 8 + i) * LO
                width = min(LO, TILE_PIX - first)
                sky_ref[q : q + 1, first : first + width] = stokes[q][i : i + 1, :width]

    def look(run, group, r, first, fresh):
        pixel = chunk_row(pix_ref, run, group, r)
        start = pl.multiple_of(first * 8, 8)
        planes = [x for q in range(3) for x in split2(sum_ref[q, pl.ds(start, WIN), :])]
        found = lax.dot_general(
            jnp.concatenate(planes, axis=0).astype(BF16),
            one_hot_cols(pixel & (LO - 1), LO),
            NN,
            preferred_element_type=F32,
        )
        stokes = [
            found[2 * q * WIN : (2 * q + 1) * WIN] + found[(2 * q + 1) * WIN : (2 * q + 2) * WIN]
            for q in range(3)
        ]
        cosine = chunk_row(cos_ref, run, group, r)
        sine = chunk_row(sin_ref, run, group, r)
        signal = stokes[0] + cosine * stokes[1] + sine * stokes[2]
        here = (iota(signal.shape, 0) + start) == (pixel >> 8)
        value = jnp.sum(jnp.where(here, signal, 0.0), axis=0, keepdims=True)
        for i in range(GROUP):
            part = value[:, i * LANES : (i + 1) * LANES]
            if fresh:
                parts_ref[0, run, GROUP * group + i, r : r + 1, :] = part
            else:
                parts_ref[0, run, GROUP * group + i, r : r + 1, :] += part

    over_chunks(groups, rows, table, look)

    for at in range(owners // WAYS):
        mixed = shuffle([parts_ref[0, run, at] for run in range(WAYS)], lane)
        for i in range(WAYS):
            back_ref[at * WAYS + i] = mixed[i]


def make_map(got, mixed):
    rows = got.shape[1]
    return pl.pallas_call(
        map_kernel,
        out_shape=(
            jax.ShapeDtypeStruct((3, TILE_PIX), F32),
            jax.ShapeDtypeStruct(got.shape, F32),
        ),
        in_specs=[VMEM_SPEC, VMEM_SPEC],
        out_specs=(VMEM_SPEC, VMEM_SPEC),
        scratch_shapes=[
            pltpu.VMEM(mixed.shape[1:], jnp.int32),
            pltpu.VMEM((PARTS,) + mixed.shape[1:], F32),
            pltpu.VMEM((8, HIP, LO), F32),
            pltpu.VMEM((rows, LANES), jnp.int32),
            pltpu.SMEM((rows, LANES), jnp.int32),
            pltpu.SemaphoreType.DMA,
        ],
        compiler_params=pltpu.CompilerParams(vmem_limit_bytes=VMEM_LIMIT),
        name="make_map",
    )(got, mixed)


def residual_kernel(got_ref, idx_ref, clean_ref, out_ref):
    det_local, length = clean_ref.shape
    owners, rows = idx_ref.shape[0], idx_ref.shape[1]
    det_id = iota((det_local, 2 * LANES), 0)

    def step(pair, total):
        for r in range(rows):
            index = jnp.concatenate(
                [idx_ref[2 * pair, r : r + 1, :], idx_ref[2 * pair + 1, r : r + 1, :]], axis=1
            )
            value = jnp.concatenate(
                [got_ref[2 * pair, r : r + 1, :], got_ref[2 * pair + 1, r : r + 1, :]], axis=1
            )
            here = det_id == index // length
            stacked = [
                jnp.where(here, jnp.broadcast_to(piece, here.shape), 0.0) for piece in split2(value)
            ]
            total = total + lax.dot_general(
                jnp.concatenate(stacked, axis=0).astype(BF16),
                one_hot_cols(index & (length - 1), length),
                NT,
                preferred_element_type=F32,
            )
        return total

    total = lax.fori_loop(
        0, owners // 2, step, jnp.zeros((2 * det_local, length), F32), unroll=4
    )
    signal = total[:det_local] + total[det_local:]
    out_ref[...] = clean_ref[...] - signal


def residuals(got, idx, cleaned):
    return pl.pallas_call(
        residual_kernel,
        out_shape=jax.ShapeDtypeStruct(cleaned.shape, F32),
        in_specs=[VMEM_SPEC] * 3,
        out_specs=VMEM_SPEC,
        compiler_params=pltpu.CompilerParams(vmem_limit_bytes=VMEM_LIMIT),
        name="residuals",
    )(got, idx, cleaned)


def shards(timestream, tile_index, pixel_index, angle_bin, owner_map):
    blocks, det_local, sample_local = timestream.shape
    samples = timestream[0]
    tm_count = lax.axis_size("tm")
    det_count = lax.axis_size("det")
    owners = tm_count * det_count
    flat = det_local * sample_local
    rows = flat // (owners // 2) // LANES

    parts = [samples] + [
        lax.ppermute(samples, "det", [(i, (i + k) % det_count) for i in range(det_count)])
        for k in range(1, det_count)
    ]
    def flatten(x):
        x = x.reshape(det_local // 8, 8, sample_local // LANES, LANES)
        return x.transpose(0, 2, 1, 3).reshape(flat)

    number = jnp.arange(flat, dtype=jnp.int32).reshape(tile_index.shape)
    key = flatten((tile_index << PIX_BITS) + pixel_index)
    load = flatten((number << 10) + angle_bin)
    key, load = lax.sort((key, load), num_keys=1, is_stable=False)
    key, load, parts = lax.optimization_barrier((key, load, parts))
    templates, products = modes(parts, det_local * det_count // MODES, tm_count)
    products = lax.all_to_all(products, "tm", split_axis=0, concat_axis=0, tiled=True)
    send, idx = route(key, load, owner_map, owners, rows)
    everywhere = functools.partial(
        lax.all_to_all, axis_name=("tm", "det"), split_axis=0, concat_axis=0, tiled=True
    )
    got = everywhere(send)
    cleaned, pay = clean(products, templates, samples, idx)
    mixed = prepare(got, rows)

    values = everywhere(pay)
    sky, back = make_map(values, mixed)
    residual = residuals(everywhere(back), idx, cleaned)
    return (sky, residual.reshape(blocks, det_local, sample_local))


def solution(mesh):
    placed = (
        P("tm", "det", None),
        P("tm", "det", None),
        P("tm", "det", None),
        P("tm", "det", None),
        P(),
    )
    return jax.shard_map(
        shards,
        mesh=mesh,
        in_specs=placed,
        out_specs=(P(None, ("tm", "det")), P("tm", "det", None)),
        check_vma=False,
    )
```

```python
import functools

import jax
import jax.numpy as jnp
from jax import lax
from jax.experimental import pallas as pl
from jax.experimental.pallas import tpu as pltpu
from jax.sharding import PartitionSpec as P

MODES = 16
NBINS = 1024
TILE_PIX = 32640
RIDGE = 1.0
LANES = 128
LO = 256
HI = -(-TILE_PIX // LO)
WIN = 32
HIP = HI + WIN - 8
SUB = 32
WAYS = LANES // SUB
GROUP = 8
PIX_BITS = 15
HALF = LANES // 2
F32 = jnp.float32
BF16 = jnp.bfloat16
HIGHEST = lax.Precision.HIGHEST
NT = (((1,), (1,)), ((), ()))
NN = (((1,), (0,)), ((), ()))
VMEM_LIMIT = 24 * 1024 * 1024
VMEM_SPEC = pl.BlockSpec(memory_space=pltpu.VMEM)


def iota(shape, dim):
    return lax.broadcasted_iota(jnp.int32, shape, dim)


def split3(x):
    first = x.astype(BF16).astype(F32)
    rest = x - first
    second = rest.astype(BF16).astype(F32)
    return first, second, rest - second


def split2(x):
    return split3(x)[:2]


def one_hot_cols(row, rows):
    ids = iota((rows, row.shape[1]), 0).astype(F32).astype(BF16)
    want = jnp.broadcast_to(row.astype(F32).astype(BF16), ids.shape)
    return jnp.where(ids == want, jnp.ones_like(ids), jnp.zeros_like(ids))


def modes_kernel(members, *refs):
    part_refs = refs[:-2]
    temp_ref, out_ref = refs[-2:]
    own_ref = part_refs[0]
    groups = own_ref.shape[0] // MODES
    templates = sum(ref[g * MODES : (g + 1) * MODES, :] for ref in part_refs for g in range(groups))
    templates = templates / members
    temp_ref[...] = templates
    both = jnp.concatenate([templates, own_ref[...]], axis=0)
    products = lax.dot_general(templates, both, NT, precision=HIGHEST, preferred_element_type=F32)
    pad = jnp.zeros((MODES, HALF - products.shape[1]), F32)
    half = jnp.concatenate([products, pad], axis=1)
    out_ref[...] = jnp.concatenate([half[: MODES // 2], half[MODES // 2 :]], axis=1)


def modes(parts, members):
    return pl.pallas_call(
        functools.partial(modes_kernel, members),
        out_shape=(
            jax.ShapeDtypeStruct((MODES, parts[0].shape[1]), F32),
            jax.ShapeDtypeStruct((MODES // 2, LANES), F32),
        ),
        in_specs=[VMEM_SPEC] * len(parts),
        out_specs=(VMEM_SPEC, VMEM_SPEC),
        compiler_params=pltpu.CompilerParams(vmem_limit_bytes=VMEM_LIMIT),
        name="modes",
    )(*parts)


def route_kernel(owner_ref, key_ref, load_ref, send_ref, idx_ref, keys, loads):
    tiles, rows = idx_ref.shape[0], idx_ref.shape[1]
    depth = key_ref.shape[0]
    keys[0:depth, :] = key_ref[...]
    loads[0:depth, :] = load_ref[...]
    keys[depth:, :] = jnp.zeros((8, LANES), jnp.int32)
    loads[depth:, :] = jnp.zeros((8, LANES), jnp.int32)
    sorted_keys = key_ref[...]
    lane = iota((8, LANES), 1)
    slot = iota((8, LANES), 0) * LANES + lane
    starts = [jnp.int32(0)]
    for tile in range(1, tiles):
        below = (sorted_keys < (tile << PIX_BITS)).astype(F32)
        starts.append(jnp.sum(below).astype(jnp.int32))
    starts.append(jnp.int32(depth * LANES))
    for tile in range(tiles):
        start = starts[tile]
        count = starts[tile + 1] - start
        top = start // LANES
        shift = start % LANES
        back = lax.rem(LANES - shift, LANES)
        whole = lane < LANES - shift

        def run(ref):
            turned = pltpu.roll(ref[pl.ds(top, 8), :], back, 1)
            return jnp.where(whole, turned, pltpu.roll(turned, 7, 0))

        key = run(keys)
        load = run(loads)
        live = slot < count
        owner = owner_ref[tile]
        pixel = jnp.where(live, key & ((1 << PIX_BITS) - 1), -1)
        index = jnp.where(live, load >> 10, -1)
        send_ref[owner, 0:rows, :] = pixel[0:rows]
        send_ref[owner, rows : 2 * rows, :] = (load & (NBINS - 1))[0:rows]
        idx_ref[owner, :, :] = index[0:rows]


def route(key, load, owner_map, owners, rows):
    flat = key.shape[0]
    depth = flat // LANES
    return pl.pallas_call(
        route_kernel,
        out_shape=(
            jax.ShapeDtypeStruct((owners, 2 * rows, LANES), jnp.int32),
            jax.ShapeDtypeStruct((owners, rows, LANES), jnp.int32),
        ),
        in_specs=[pl.BlockSpec(memory_space=pltpu.SMEM), VMEM_SPEC, VMEM_SPEC],
        out_specs=(VMEM_SPEC, VMEM_SPEC),
        scratch_shapes=[
            pltpu.VMEM((depth + 8, LANES), jnp.int32),
            pltpu.VMEM((depth + 8, LANES), jnp.int32),
        ],
        compiler_params=pltpu.CompilerParams(vmem_limit_bytes=VMEM_LIMIT),
        name="route",
    )(owner_map, key.reshape(depth, LANES), load.reshape(depth, LANES))


def clean_kernel(temp_ref, samples_ref, idx_ref, *refs):
    clean_ref, pay_ref = refs[-2:]
    det_local, length = samples_ref.shape
    owners, rows = idx_ref.shape[0], idx_ref.shape[1]
    packed = sum(ref[...] for ref in refs[:-2])
    system = jnp.concatenate([packed, pltpu.roll(packed, HALF, 1)], axis=0)
    row_id = iota((MODES, LANES), 0)
    lane_id = iota((MODES, LANES), 1)
    system = system + jnp.where(row_id == lane_id, RIDGE, 0.0)
    for k in range(MODES):
        pivot = system[k : k + 1, :] / system[k : k + 1, k : k + 1]
        column = system[:, k : k + 1]
        system = jnp.where(row_id == k, pivot, system - column * pivot)
    coef = system[:, MODES : MODES + det_local]
    model = lax.dot_general(
        coef, temp_ref[...], (((0,), (0,)), ((), ())), precision=HIGHEST, preferred_element_type=F32
    )
    cleaned = samples_ref[...] - model
    clean_ref[...] = cleaned
    parts = jnp.concatenate(split2(cleaned), axis=0).astype(BF16)
    det_id = iota((det_local, 2 * LANES), 0)

    def step(pair, _):
        for r in range(rows):
            index = jnp.concatenate(
                [idx_ref[2 * pair, r : r + 1, :], idx_ref[2 * pair + 1, r : r + 1, :]], axis=1
            )
            picked = lax.dot_general(
                parts, one_hot_cols(index & (length - 1), length), NN, preferred_element_type=F32
            )
            total = picked[:det_local] + picked[det_local:]
            here = jnp.where(det_id == index // length, total, 0.0)
            value = jnp.sum(here, axis=0, keepdims=True)
            pay_ref[2 * pair, r : r + 1, :] = value[:, :LANES]
            pay_ref[2 * pair + 1, r : r + 1, :] = value[:, LANES:]
        return 0

    lax.fori_loop(0, owners // 2, step, 0, unroll=4)


def clean(sums, templates, samples, idx):
    return pl.pallas_call(
        clean_kernel,
        out_shape=(
            jax.ShapeDtypeStruct(samples.shape, F32),
            jax.ShapeDtypeStruct(idx.shape, F32),
        ),
        in_specs=[VMEM_SPEC] * (3 + len(sums)),
        out_specs=(VMEM_SPEC, VMEM_SPEC),
        compiler_params=pltpu.CompilerParams(vmem_limit_bytes=VMEM_LIMIT),
        name="clean",
    )(templates, samples, idx, *sums)


def shuffle(blocks, lane):
    blocks = list(blocks)
    width = HALF
    while width >= SUB:
        low = (lane & width) == 0
        step = width // SUB
        for i in range(WAYS):
            if i & step == 0:
                a, b = blocks[i], blocks[i + step]
                blocks[i] = jnp.where(low, a, pltpu.roll(b, width, 1))
                blocks[i + step] = jnp.where(low, pltpu.roll(a, LANES - width, 1), b)
        width //= 2
    return blocks


def chunk_row(ref, run, group, r):
    return jnp.concatenate([ref[run, GROUP * group + i, r : r + 1, :] for i in range(GROUP)], axis=1)


def over_chunks(groups, rows, table_ref, body):
    def step(i, _):
        run, group = lax.rem(i, WAYS), lax.div(i, WAYS)
        ends = [(table_ref[r, 2 * i], table_ref[r, 2 * i + 1]) for r in range(rows)]
        widest = functools.reduce(jnp.maximum, [high - low for low, high in ends])

        for r in range(rows):
            body(run, group, r, ends[r][0], True)

        @pl.when(widest >= WIN // 8)
        def _():
            for r in range(rows):
                low, high = ends[r]

                def more(w, _):
                    body(run, group, r, low + w * (WIN // 8), False)
                    return 0

                lax.fori_loop(1, (high - low) // (WIN // 8) + 1, more, 0)

        return 0

    lax.fori_loop(0, groups * WAYS, step, 0)


def windows_of(pix_ref, groups, rows):
    table_lane = iota((rows, LANES), 1)
    windows = jnp.zeros((rows, LANES), jnp.int32)
    for group in range(groups):
        for run in range(WAYS):
            ends = [pix_ref[run, group * GROUP + i] for i in range(GROUP)]
            most = functools.reduce(jnp.maximum, ends)
            least = functools.reduce(
                jnp.minimum, [jnp.where(x < 0, TILE_PIX - 1, x) for x in ends]
            )
            most = jnp.max(most, axis=1, keepdims=True)
            least = jnp.min(least, axis=1, keepdims=True)
            high = most >> 11
            low = jnp.where(most < 0, 0, least >> 11)
            at = 2 * (group * WAYS + run)
            windows = jnp.where(table_lane == at, low, windows)
            windows = jnp.where(table_lane == at + 1, high, windows)
    return windows


def scatter_add(sum_ref, terms, pieces, pixel, first):
    start = pl.multiple_of(first * 8, 8)
    here = (iota((WIN, pixel.shape[1]), 0) + start) == (pixel >> 8)
    stacked = [jnp.where(here, jnp.broadcast_to(x, here.shape), 0.0) for x in pieces]
    found = lax.dot_general(
        jnp.concatenate(stacked, axis=0).astype(BF16),
        one_hot_cols(pixel & (LO - 1), LO),
        NT,
        preferred_element_type=F32,
    )
    at = 0
    for q, count in enumerate(terms):
        total = found[at : at + WIN]
        for i in range(1, count):
            total = total + found[at + i * WIN : at + (i + 1) * WIN]
        at += count * WIN
        sum_ref[q, pl.ds(start, WIN), :] += total


ANGLE_TERMS = (1, 3, 3, 3, 3)
VALUE_TERMS = (2, 3, 3)


def angles_kernel(got_ref, mixed_ref, sum_ref, pix_ref, parts_ref, table_vmem, table, sem):
    owners, rows = got_ref.shape[0], mixed_ref.shape[3]
    groups = owners // WAYS // GROUP
    lane = iota((2 * rows, LANES), 1)
    for at in range(owners // WAYS):
        mixed = shuffle([got_ref[at * WAYS + i] for i in range(WAYS)], lane)
        for run in range(WAYS):
            pix_ref[run, at] = mixed[run][:rows]
            mixed_ref[0, run, at] = mixed[run][:rows].astype(F32)
    table_vmem[...] = windows_of(pix_ref, groups, rows)
    copy = pltpu.make_async_copy(table_vmem, table, sem)
    copy.start()
    for at in range(owners // WAYS):
        mixed = shuffle([got_ref[at * WAYS + i] for i in range(WAYS)], lane)
        for run in range(WAYS):
            angle = (jnp.pi * mixed[run][rows:].astype(F32) / NBINS) * 2.0
            cosine, sine = jnp.cos(angle), jnp.sin(angle)
            mixed_ref[1, run, at] = cosine
            mixed_ref[2, run, at] = sine
            parts = (
                split3(cosine) + split3(sine) + split3(cosine * cosine) + split3(cosine * sine)
            )
            for p, part in enumerate(parts):
                parts_ref[p, run, at] = part
    sum_ref[...] = jnp.zeros_like(sum_ref)
    copy.wait()

    def add(run, group, r, first, _):
        pixel = chunk_row(pix_ref, run, group, r)
        pieces = [jnp.ones(pixel.shape, F32)]
        pieces += [chunk_row(parts_ref.at[p], run, group, r) for p in range(parts_ref.shape[0])]
        scatter_add(sum_ref, ANGLE_TERMS, pieces, pixel, first)

    over_chunks(groups, rows, table, add)


def angles(got, rows):
    mixed = (WAYS, got.shape[0] // WAYS, rows, LANES)
    return pl.pallas_call(
        angles_kernel,
        out_shape=(
            jax.ShapeDtypeStruct((3,) + mixed, F32),
            jax.ShapeDtypeStruct((len(ANGLE_TERMS), HIP, LO), F32),
        ),
        in_specs=[VMEM_SPEC],
        out_specs=(VMEM_SPEC, VMEM_SPEC),
        scratch_shapes=[
            pltpu.VMEM(mixed, jnp.int32),
            pltpu.VMEM((sum(ANGLE_TERMS) - 1,) + mixed, F32),
            pltpu.VMEM((rows, LANES), jnp.int32),
            pltpu.SMEM((rows, LANES), jnp.int32),
            pltpu.SemaphoreType.DMA,
        ],
        compiler_params=pltpu.CompilerParams(vmem_limit_bytes=VMEM_LIMIT),
        name="angles",
    )(got)


def solve_stokes(sums):
    a11 = sums[0] + RIDGE
    a12 = sums[1]
    a13 = sums[2]
    a22 = sums[3] + RIDGE
    a23 = sums[4]
    a33 = sums[5] + RIDGE
    c11 = a22 * a33 - a23 * a23
    c12 = a13 * a23 - a12 * a33
    c13 = a12 * a23 - a13 * a22
    c22 = a11 * a33 - a13 * a13
    c23 = a12 * a13 - a11 * a23
    c33 = a11 * a22 - a12 * a12
    inverse = 1.0 / (a11 * c11 + a12 * c12 + a13 * c13)
    stokes_i = (c11 * sums[6] + c12 * sums[7] + c13 * sums[8]) * inverse
    stokes_q = (c12 * sums[6] + c22 * sums[7] + c23 * sums[8]) * inverse
    stokes_u = (c13 * sums[6] + c23 * sums[7] + c33 * sums[8]) * inverse
    return (stokes_i, stokes_q, stokes_u)


def map_kernel(
    got_ref, mixed_ref, acc_ref, sky_ref, back_ref, pix_ref, parts_ref, sum_ref, table_vmem, table, sem
):
    owners, rows = got_ref.shape[0], got_ref.shape[1]
    groups = owners // WAYS // GROUP
    lane = iota((rows, LANES), 1)
    cos_ref, sin_ref = mixed_ref.at[1], mixed_ref.at[2]
    pix_ref[...] = mixed_ref[0].astype(jnp.int32)
    table_vmem[...] = windows_of(pix_ref, groups, rows)
    copy = pltpu.make_async_copy(table_vmem, table, sem)
    copy.start()
    for at in range(owners // WAYS):
        mixed = shuffle([got_ref[at * WAYS + i] for i in range(WAYS)], lane)
        for run in range(WAYS):
            value, cosine, sine = mixed[run], cos_ref[run, at], sin_ref[run, at]
            parts = split2(value) + split3(cosine * value) + split3(sine * value)
            for p, part in enumerate(parts):
                parts_ref[p, run, at] = part
    sum_ref[...] = jnp.zeros_like(sum_ref)
    copy.wait()

    def add(run, group, r, first, _):
        pixel = chunk_row(pix_ref, run, group, r)
        pieces = [chunk_row(parts_ref.at[p], run, group, r) for p in range(parts_ref.shape[0])]
        scatter_add(sum_ref, VALUE_TERMS, pieces, pixel, first)

    over_chunks(groups, rows, table, add)

    for block in range(HI // 8):
        at = pl.ds(block * 8, 8)
        sums = [acc_ref[q, at, :] for q in range(5)]
        sums += [sums[0] - sums[3]] + [sum_ref[q, at, :] for q in range(3)]
        stokes = solve_stokes(sums)
        for q in range(3):
            sum_ref[q, at, :] = stokes[q]
            for i in range(8):
                first = (block * 8 + i) * LO
                width = min(LO, TILE_PIX - first)
                sky_ref[q : q + 1, first : first + width] = stokes[q][i : i + 1, :width]

    def look(run, group, r, first, fresh):
        pixel = chunk_row(pix_ref, run, group, r)
        start = pl.multiple_of(first * 8, 8)
        planes = [x for q in range(3) for x in split2(sum_ref[q, pl.ds(start, WIN), :])]
        found = lax.dot_general(
            jnp.concatenate(planes, axis=0).astype(BF16),
            one_hot_cols(pixel & (LO - 1), LO),
            NN,
            preferred_element_type=F32,
        )
        stokes = [
            found[2 * q * WIN : (2 * q + 1) * WIN] + found[(2 * q + 1) * WIN : (2 * q + 2) * WIN]
            for q in range(3)
        ]
        cosine = chunk_row(cos_ref, run, group, r)
        sine = chunk_row(sin_ref, run, group, r)
        signal = stokes[0] + cosine * stokes[1] + sine * stokes[2]
        here = (iota(signal.shape, 0) + start) == (pixel >> 8)
        value = jnp.sum(jnp.where(here, signal, 0.0), axis=0, keepdims=True)
        for i in range(GROUP):
            part = value[:, i * LANES : (i + 1) * LANES]
            if fresh:
                parts_ref[0, run, GROUP * group + i, r : r + 1, :] = part
            else:
                parts_ref[0, run, GROUP * group + i, r : r + 1, :] += part

    over_chunks(groups, rows, table, look)

    for at in range(owners // WAYS):
        mixed = shuffle([parts_ref[0, run, at] for run in range(WAYS)], lane)
        for i in range(WAYS):
            back_ref[at * WAYS + i] = mixed[i]


def make_map(got, mixed, acc):
    rows = got.shape[1]
    return pl.pallas_call(
        map_kernel,
        out_shape=(
            jax.ShapeDtypeStruct((3, TILE_PIX), F32),
            jax.ShapeDtypeStruct(got.shape, F32),
        ),
        in_specs=[VMEM_SPEC] * 3,
        out_specs=(VMEM_SPEC, VMEM_SPEC),
        scratch_shapes=[
            pltpu.VMEM(mixed.shape[1:], jnp.int32),
            pltpu.VMEM((sum(VALUE_TERMS),) + mixed.shape[1:], F32),
            pltpu.VMEM((len(VALUE_TERMS), HIP, LO), F32),
            pltpu.VMEM((rows, LANES), jnp.int32),
            pltpu.SMEM((rows, LANES), jnp.int32),
            pltpu.SemaphoreType.DMA,
        ],
        compiler_params=pltpu.CompilerParams(vmem_limit_bytes=VMEM_LIMIT),
        name="make_map",
    )(got, mixed, acc)


def residual_kernel(got_ref, idx_ref, clean_ref, out_ref):
    det_local, length = clean_ref.shape
    owners, rows = idx_ref.shape[0], idx_ref.shape[1]
    det_id = iota((det_local, 2 * LANES), 0)

    def step(pair, total):
        for r in range(rows):
            index = jnp.concatenate(
                [idx_ref[2 * pair, r : r + 1, :], idx_ref[2 * pair + 1, r : r + 1, :]], axis=1
            )
            value = jnp.concatenate(
                [got_ref[2 * pair, r : r + 1, :], got_ref[2 * pair + 1, r : r + 1, :]], axis=1
            )
            here = det_id == index // length
            stacked = [
                jnp.where(here, jnp.broadcast_to(piece, here.shape), 0.0) for piece in split2(value)
            ]
            total = total + lax.dot_general(
                jnp.concatenate(stacked, axis=0).astype(BF16),
                one_hot_cols(index & (length - 1), length),
                NT,
                preferred_element_type=F32,
            )
        return total

    total = lax.fori_loop(
        0, owners // 2, step, jnp.zeros((2 * det_local, length), F32), unroll=4
    )
    signal = total[:det_local] + total[det_local:]
    out_ref[...] = clean_ref[...] - signal


def residuals(got, idx, cleaned):
    return pl.pallas_call(
        residual_kernel,
        out_shape=jax.ShapeDtypeStruct(cleaned.shape, F32),
        in_specs=[VMEM_SPEC] * 3,
        out_specs=VMEM_SPEC,
        compiler_params=pltpu.CompilerParams(vmem_limit_bytes=VMEM_LIMIT),
        name="residuals",
    )(got, idx, cleaned)


def shards(timestream, tile_index, pixel_index, angle_bin, owner_map):
    blocks, det_local, sample_local = timestream.shape
    samples = timestream[0]
    tm_count = lax.axis_size("tm")
    det_count = lax.axis_size("det")
    owners = tm_count * det_count
    flat = det_local * sample_local
    rows = flat // (owners // 2) // LANES

    parts = [samples] + [
        lax.ppermute(samples, "det", [(i, (i + k) % det_count) for i in range(det_count)])
        for k in range(1, det_count)
    ]
    def flatten(x):
        x = x.reshape(det_local // 8, 8, sample_local // LANES, LANES)
        return x.transpose(0, 2, 1, 3).reshape(flat)

    number = jnp.arange(flat, dtype=jnp.int32).reshape(tile_index.shape)
    key = flatten((tile_index << PIX_BITS) + pixel_index)
    load = flatten((number << 10) + angle_bin)
    key, load = lax.sort((key, load), num_keys=1, is_stable=False)
    key, load, parts = lax.optimization_barrier((key, load, parts))
    templates, products = modes(parts, det_local * det_count // MODES)
    key, load, products = lax.optimization_barrier((key, load, products))
    send, idx = route(key, load, owner_map, owners, rows)
    products = products + lax.ppermute(products, "tm", [(i, i ^ 1) for i in range(tm_count)])
    products, send = lax.optimization_barrier((products, send))
    products = [products] + [
        lax.ppermute(products, "tm", [(i, (i + k) % tm_count) for i in range(tm_count)])
        for k in range(2, tm_count, 2)
    ]
    everywhere = functools.partial(
        lax.all_to_all, axis_name=("tm", "det"), split_axis=0, concat_axis=0, tiled=True
    )
    got = everywhere(send)
    cleaned, pay = clean(products, templates, samples, idx)
    mixed, acc = angles(got, rows)

    values = everywhere(pay)
    sky, back = make_map(values, mixed, acc)
    residual = residuals(everywhere(back), idx, cleaned)
    return (sky, residual.reshape(blocks, det_local, sample_local))


def solution(mesh):
    placed = (
        P("tm", "det", None),
        P("tm", "det", None),
        P("tm", "det", None),
        P("tm", "det", None),
        P(),
    )
    return jax.shard_map(
        shards,
        mesh=mesh,
        in_specs=placed,
        out_specs=(P(None, ("tm", "det")), P("tm", "det", None)),
        check_vma=False,
    )
```

```python
import functools

import jax
import jax.numpy as jnp
from jax import lax
from jax.experimental import pallas as pl
from jax.experimental.pallas import tpu as pltpu
from jax.sharding import PartitionSpec as P

MODES = 16
NBINS = 1024
TILE_PIX = 32640
RIDGE = 1.0
LANES = 128
LO = 256
HI = -(-TILE_PIX // LO)
WIN = 32
HIP = HI + WIN - 8
SUB = 32
WAYS = LANES // SUB
GROUP = 8
PIX_BITS = 15
HALF = LANES // 2
F32 = jnp.float32
BF16 = jnp.bfloat16
HIGHEST = lax.Precision.HIGHEST
NT = (((1,), (1,)), ((), ()))
NN = (((1,), (0,)), ((), ()))
VMEM_LIMIT = 24 * 1024 * 1024
VMEM_SPEC = pl.BlockSpec(memory_space=pltpu.VMEM)


def iota(shape, dim):
    return lax.broadcasted_iota(jnp.int32, shape, dim)


def split3(x):
    first = x.astype(BF16).astype(F32)
    rest = x - first
    second = rest.astype(BF16).astype(F32)
    return first, second, rest - second


def split2(x):
    return split3(x)[:2]


def one_hot_cols(row, rows):
    ids = iota((rows, row.shape[1]), 0).astype(F32).astype(BF16)
    want = jnp.broadcast_to(row.astype(F32).astype(BF16), ids.shape)
    return jnp.where(ids == want, jnp.ones_like(ids), jnp.zeros_like(ids))


def modes_kernel(members, *refs):
    part_refs = refs[:-2]
    temp_ref, out_ref = refs[-2:]
    own_ref = part_refs[0]
    groups = own_ref.shape[0] // MODES
    templates = sum(ref[g * MODES : (g + 1) * MODES, :] for ref in part_refs for g in range(groups))
    templates = templates / members
    temp_ref[...] = templates
    both = jnp.concatenate([templates, own_ref[...]], axis=0)
    products = lax.dot_general(templates, both, NT, precision=HIGHEST, preferred_element_type=F32)
    pad = jnp.zeros((MODES, HALF - products.shape[1]), F32)
    half = jnp.concatenate([products, pad], axis=1)
    out_ref[...] = jnp.concatenate([half[: MODES // 2], half[MODES // 2 :]], axis=1)


def modes(parts, members):
    return pl.pallas_call(
        functools.partial(modes_kernel, members),
        out_shape=(
            jax.ShapeDtypeStruct((MODES, parts[0].shape[1]), F32),
            jax.ShapeDtypeStruct((MODES // 2, LANES), F32),
        ),
        in_specs=[VMEM_SPEC] * len(parts),
        out_specs=(VMEM_SPEC, VMEM_SPEC),
        compiler_params=pltpu.CompilerParams(vmem_limit_bytes=VMEM_LIMIT),
        name="modes",
    )(*parts)


def route_kernel(owner_ref, key_ref, load_ref, send_ref, idx_ref, keys, loads):
    tiles, rows = idx_ref.shape[0], idx_ref.shape[1]
    depth = key_ref.shape[0]
    keys[0:depth, :] = key_ref[...]
    loads[0:depth, :] = load_ref[...]
    keys[depth:, :] = jnp.zeros((8, LANES), jnp.int32)
    loads[depth:, :] = jnp.zeros((8, LANES), jnp.int32)
    sorted_keys = key_ref[...]
    lane = iota((8, LANES), 1)
    slot = iota((8, LANES), 0) * LANES + lane
    starts = [jnp.int32(0)]
    for tile in range(1, tiles):
        below = (sorted_keys < (tile << PIX_BITS)).astype(F32)
        starts.append(jnp.sum(below).astype(jnp.int32))
    starts.append(jnp.int32(depth * LANES))
    for tile in range(tiles):
        start = starts[tile]
        count = starts[tile + 1] - start
        top = start // LANES
        shift = start % LANES
        back = lax.rem(LANES - shift, LANES)
        whole = lane < LANES - shift

        def run(ref):
            turned = pltpu.roll(ref[pl.ds(top, 8), :], back, 1)
            return jnp.where(whole, turned, pltpu.roll(turned, 7, 0))

        key = run(keys)
        load = run(loads)
        live = slot < count
        owner = owner_ref[tile]
        pixel = jnp.where(live, key & ((1 << PIX_BITS) - 1), -1)
        index = jnp.where(live, load >> 10, -1)
        send_ref[owner, 0:rows, :] = pixel[0:rows]
        send_ref[owner, rows : 2 * rows, :] = (load & (NBINS - 1))[0:rows]
        idx_ref[owner, :, :] = index[0:rows]


def route(key, load, owner_map, owners, rows):
    flat = key.shape[0]
    depth = flat // LANES
    return pl.pallas_call(
        route_kernel,
        out_shape=(
            jax.ShapeDtypeStruct((owners, 2 * rows, LANES), jnp.int32),
            jax.ShapeDtypeStruct((owners, rows, LANES), jnp.int32),
        ),
        in_specs=[pl.BlockSpec(memory_space=pltpu.SMEM), VMEM_SPEC, VMEM_SPEC],
        out_specs=(VMEM_SPEC, VMEM_SPEC),
        scratch_shapes=[
            pltpu.VMEM((depth + 8, LANES), jnp.int32),
            pltpu.VMEM((depth + 8, LANES), jnp.int32),
        ],
        compiler_params=pltpu.CompilerParams(vmem_limit_bytes=VMEM_LIMIT),
        name="route",
    )(owner_map, key.reshape(depth, LANES), load.reshape(depth, LANES))


def clean_kernel(temp_ref, samples_ref, idx_ref, *refs):
    clean_ref, pay_ref = refs[-2:]
    det_local, length = samples_ref.shape
    owners, rows = idx_ref.shape[0], idx_ref.shape[1]
    packed = sum(ref[...] for ref in refs[:-2])
    system = jnp.concatenate([packed, pltpu.roll(packed, HALF, 1)], axis=0)
    row_id = iota((MODES, LANES), 0)
    lane_id = iota((MODES, LANES), 1)
    system = system + jnp.where(row_id == lane_id, RIDGE, 0.0)
    for k in range(MODES):
        pivot = system[k : k + 1, :] / system[k : k + 1, k : k + 1]
        column = system[:, k : k + 1]
        system = jnp.where(row_id == k, pivot, system - column * pivot)
    coef = system[:, MODES : MODES + det_local]
    model = lax.dot_general(
        coef, temp_ref[...], (((0,), (0,)), ((), ())), precision=HIGHEST, preferred_element_type=F32
    )
    cleaned = samples_ref[...] - model
    clean_ref[...] = cleaned
    parts = jnp.concatenate(split2(cleaned), axis=0).astype(BF16)
    det_id = iota((det_local, 2 * LANES), 0)

    def step(pair, _):
        for r in range(rows):
            index = jnp.concatenate(
                [idx_ref[2 * pair, r : r + 1, :], idx_ref[2 * pair + 1, r : r + 1, :]], axis=1
            )
            picked = lax.dot_general(
                parts, one_hot_cols(index & (length - 1), length), NN, preferred_element_type=F32
            )
            total = picked[:det_local] + picked[det_local:]
            here = jnp.where(det_id == index // length, total, 0.0)
            value = jnp.sum(here, axis=0, keepdims=True)
            pay_ref[2 * pair, r : r + 1, :] = value[:, :LANES]
            pay_ref[2 * pair + 1, r : r + 1, :] = value[:, LANES:]
        return 0

    lax.fori_loop(0, owners // 2, step, 0, unroll=16)


def clean(sums, templates, samples, idx):
    return pl.pallas_call(
        clean_kernel,
        out_shape=(
            jax.ShapeDtypeStruct(samples.shape, F32),
            jax.ShapeDtypeStruct(idx.shape, F32),
        ),
        in_specs=[VMEM_SPEC] * (3 + len(sums)),
        out_specs=(VMEM_SPEC, VMEM_SPEC),
        compiler_params=pltpu.CompilerParams(vmem_limit_bytes=VMEM_LIMIT),
        name="clean",
    )(templates, samples, idx, *sums)


def shuffle(blocks, lane):
    blocks = list(blocks)
    width = HALF
    while width >= SUB:
        low = (lane & width) == 0
        step = width // SUB
        for i in range(WAYS):
            if i & step == 0:
                a, b = blocks[i], blocks[i + step]
                blocks[i] = jnp.where(low, a, pltpu.roll(b, width, 1))
                blocks[i + step] = jnp.where(low, pltpu.roll(a, LANES - width, 1), b)
        width //= 2
    return blocks


def chunk_row(ref, run, group, r):
    return jnp.concatenate([ref[run, GROUP * group + i, r : r + 1, :] for i in range(GROUP)], axis=1)


def over_chunks(groups, rows, table_ref, body):
    def step(i, _):
        run, group = lax.rem(i, WAYS), lax.div(i, WAYS)
        ends = [(table_ref[r, 2 * i], table_ref[r, 2 * i + 1]) for r in range(rows)]
        widest = functools.reduce(jnp.maximum, [high - low for low, high in ends])

        for r in range(rows):
            body(run, group, r, ends[r][0], True)

        @pl.when(widest >= WIN // 8)
        def _():
            for r in range(rows):
                low, high = ends[r]

                def more(w, _):
                    body(run, group, r, low + w * (WIN // 8), False)
                    return 0

                lax.fori_loop(1, (high - low) // (WIN // 8) + 1, more, 0)

        return 0

    lax.fori_loop(0, groups * WAYS, step, 0)


def windows_of(pix_ref, groups, rows):
    table_lane = iota((rows, LANES), 1)
    windows = jnp.zeros((rows, LANES), jnp.int32)
    for group in range(groups):
        for run in range(WAYS):
            ends = [pix_ref[run, group * GROUP + i] for i in range(GROUP)]
            most = functools.reduce(jnp.maximum, ends)
            least = functools.reduce(
                jnp.minimum, [jnp.where(x < 0, TILE_PIX - 1, x) for x in ends]
            )
            most = jnp.max(most, axis=1, keepdims=True)
            least = jnp.min(least, axis=1, keepdims=True)
            high = most >> 11
            low = jnp.where(most < 0, 0, least >> 11)
            at = 2 * (group * WAYS + run)
            windows = jnp.where(table_lane == at, low, windows)
            windows = jnp.where(table_lane == at + 1, high, windows)
    return windows


def scatter_add(sum_ref, terms, pieces, pixel, first):
    start = pl.multiple_of(first * 8, 8)
    here = (iota((WIN, pixel.shape[1]), 0) + start) == (pixel >> 8)
    stacked = [jnp.where(here, jnp.broadcast_to(x, here.shape), 0.0) for x in pieces]
    found = lax.dot_general(
        jnp.concatenate(stacked, axis=0).astype(BF16),
        one_hot_cols(pixel & (LO - 1), LO),
        NT,
        preferred_element_type=F32,
    )
    at = 0
    for q, count in enumerate(terms):
        total = found[at : at + WIN]
        for i in range(1, count):
            total = total + found[at + i * WIN : at + (i + 1) * WIN]
        at += count * WIN
        sum_ref[q, pl.ds(start, WIN), :] += total


ANGLE_TERMS = (1, 3, 3, 3, 3)
VALUE_TERMS = (2, 3, 3)


def angles_kernel(got_ref, mixed_ref, sum_ref, pix_ref, parts_ref, table_vmem, table, sem):
    owners, rows = got_ref.shape[0], mixed_ref.shape[3]
    groups = owners // WAYS // GROUP
    lane = iota((2 * rows, LANES), 1)
    for at in range(owners // WAYS):
        mixed = shuffle([got_ref[at * WAYS + i] for i in range(WAYS)], lane)
        for run in range(WAYS):
            pix_ref[run, at] = mixed[run][:rows]
            mixed_ref[0, run, at] = mixed[run][:rows].astype(F32)
    table_vmem[...] = windows_of(pix_ref, groups, rows)
    copy = pltpu.make_async_copy(table_vmem, table, sem)
    copy.start()
    for at in range(owners // WAYS):
        mixed = shuffle([got_ref[at * WAYS + i] for i in range(WAYS)], lane)
        for run in range(WAYS):
            angle = (jnp.pi * mixed[run][rows:].astype(F32) / NBINS) * 2.0
            cosine, sine = jnp.cos(angle), jnp.sin(angle)
            mixed_ref[1, run, at] = cosine
            mixed_ref[2, run, at] = sine
            parts = (
                split3(cosine) + split3(sine) + split3(cosine * cosine) + split3(cosine * sine)
            )
            for p, part in enumerate(parts):
                parts_ref[p, run, at] = part
    sum_ref[...] = jnp.zeros_like(sum_ref)
    copy.wait()

    def add(run, group, r, first, _):
        pixel = chunk_row(pix_ref, run, group, r)
        pieces = [jnp.ones(pixel.shape, F32)]
        pieces += [chunk_row(parts_ref.at[p], run, group, r) for p in range(parts_ref.shape[0])]
        scatter_add(sum_ref, ANGLE_TERMS, pieces, pixel, first)

    over_chunks(groups, rows, table, add)


def angles(got, rows):
    mixed = (WAYS, got.shape[0] // WAYS, rows, LANES)
    return pl.pallas_call(
        angles_kernel,
        out_shape=(
            jax.ShapeDtypeStruct((3,) + mixed, F32),
            jax.ShapeDtypeStruct((len(ANGLE_TERMS), HIP, LO), F32),
        ),
        in_specs=[VMEM_SPEC],
        out_specs=(VMEM_SPEC, VMEM_SPEC),
        scratch_shapes=[
            pltpu.VMEM(mixed, jnp.int32),
            pltpu.VMEM((sum(ANGLE_TERMS) - 1,) + mixed, F32),
            pltpu.VMEM((rows, LANES), jnp.int32),
            pltpu.SMEM((rows, LANES), jnp.int32),
            pltpu.SemaphoreType.DMA,
        ],
        compiler_params=pltpu.CompilerParams(vmem_limit_bytes=VMEM_LIMIT),
        name="angles",
    )(got)


def solve_stokes(sums):
    a11 = sums[0] + RIDGE
    a12 = sums[1]
    a13 = sums[2]
    a22 = sums[3] + RIDGE
    a23 = sums[4]
    a33 = sums[5] + RIDGE
    c11 = a22 * a33 - a23 * a23
    c12 = a13 * a23 - a12 * a33
    c13 = a12 * a23 - a13 * a22
    c22 = a11 * a33 - a13 * a13
    c23 = a12 * a13 - a11 * a23
    c33 = a11 * a22 - a12 * a12
    inverse = 1.0 / (a11 * c11 + a12 * c12 + a13 * c13)
    stokes_i = (c11 * sums[6] + c12 * sums[7] + c13 * sums[8]) * inverse
    stokes_q = (c12 * sums[6] + c22 * sums[7] + c23 * sums[8]) * inverse
    stokes_u = (c13 * sums[6] + c23 * sums[7] + c33 * sums[8]) * inverse
    return (stokes_i, stokes_q, stokes_u)


def map_kernel(
    got_ref, mixed_ref, acc_ref, sky_ref, back_ref, pix_ref, parts_ref, sum_ref, table_vmem, table, sem
):
    owners, rows = got_ref.shape[0], got_ref.shape[1]
    groups = owners // WAYS // GROUP
    lane = iota((rows, LANES), 1)
    cos_ref, sin_ref = mixed_ref.at[1], mixed_ref.at[2]
    pix_ref[...] = mixed_ref[0].astype(jnp.int32)
    table_vmem[...] = windows_of(pix_ref, groups, rows)
    copy = pltpu.make_async_copy(table_vmem, table, sem)
    copy.start()
    for at in range(owners // WAYS):
        mixed = shuffle([got_ref[at * WAYS + i] for i in range(WAYS)], lane)
        for run in range(WAYS):
            value, cosine, sine = mixed[run], cos_ref[run, at], sin_ref[run, at]
            parts = split2(value) + split3(cosine * value) + split3(sine * value)
            for p, part in enumerate(parts):
                parts_ref[p, run, at] = part
    sum_ref[...] = jnp.zeros_like(sum_ref)
    copy.wait()

    def add(run, group, r, first, _):
        pixel = chunk_row(pix_ref, run, group, r)
        pieces = [chunk_row(parts_ref.at[p], run, group, r) for p in range(parts_ref.shape[0])]
        scatter_add(sum_ref, VALUE_TERMS, pieces, pixel, first)

    over_chunks(groups, rows, table, add)

    for block in range(HI // 8):
        at = pl.ds(block * 8, 8)
        sums = [acc_ref[q, at, :] for q in range(5)]
        sums += [sums[0] - sums[3]] + [sum_ref[q, at, :] for q in range(3)]
        stokes = solve_stokes(sums)
        for q in range(3):
            sum_ref[q, at, :] = stokes[q]
            for i in range(8):
                first = (block * 8 + i) * LO
                width = min(LO, TILE_PIX - first)
                sky_ref[q : q + 1, first : first + width] = stokes[q][i : i + 1, :width]

    def look(run, group, r, first, fresh):
        pixel = chunk_row(pix_ref, run, group, r)
        start = pl.multiple_of(first * 8, 8)
        planes = [x for q in range(3) for x in split2(sum_ref[q, pl.ds(start, WIN), :])]
        found = lax.dot_general(
            jnp.concatenate(planes, axis=0).astype(BF16),
            one_hot_cols(pixel & (LO - 1), LO),
            NN,
            preferred_element_type=F32,
        )
        stokes = [
            found[2 * q * WIN : (2 * q + 1) * WIN] + found[(2 * q + 1) * WIN : (2 * q + 2) * WIN]
            for q in range(3)
        ]
        cosine = chunk_row(cos_ref, run, group, r)
        sine = chunk_row(sin_ref, run, group, r)
        signal = stokes[0] + cosine * stokes[1] + sine * stokes[2]
        here = (iota(signal.shape, 0) + start) == (pixel >> 8)
        value = jnp.sum(jnp.where(here, signal, 0.0), axis=0, keepdims=True)
        for i in range(GROUP):
            part = value[:, i * LANES : (i + 1) * LANES]
            if fresh:
                parts_ref[0, run, GROUP * group + i, r : r + 1, :] = part
            else:
                parts_ref[0, run, GROUP * group + i, r : r + 1, :] += part

    over_chunks(groups, rows, table, look)

    for at in range(owners // WAYS):
        mixed = shuffle([parts_ref[0, run, at] for run in range(WAYS)], lane)
        for i in range(WAYS):
            back_ref[at * WAYS + i] = mixed[i]


def make_map(got, mixed, acc):
    rows = got.shape[1]
    return pl.pallas_call(
        map_kernel,
        out_shape=(
            jax.ShapeDtypeStruct((3, TILE_PIX), F32),
            jax.ShapeDtypeStruct(got.shape, F32),
        ),
        in_specs=[VMEM_SPEC] * 3,
        out_specs=(VMEM_SPEC, VMEM_SPEC),
        scratch_shapes=[
            pltpu.VMEM(mixed.shape[1:], jnp.int32),
            pltpu.VMEM((sum(VALUE_TERMS),) + mixed.shape[1:], F32),
            pltpu.VMEM((len(VALUE_TERMS), HIP, LO), F32),
            pltpu.VMEM((rows, LANES), jnp.int32),
            pltpu.SMEM((rows, LANES), jnp.int32),
            pltpu.SemaphoreType.DMA,
        ],
        compiler_params=pltpu.CompilerParams(vmem_limit_bytes=VMEM_LIMIT),
        name="make_map",
    )(got, mixed, acc)


def invert_kernel(idx_ref, slot_ref):
    det_local, length = slot_ref.shape
    owners, rows = idx_ref.shape[0], idx_ref.shape[1]
    det_id = iota((det_local, 2 * LANES), 0)
    lane = lax.rem(iota((1, 2 * LANES), 1), LANES).astype(F32)
    second = (iota((1, 2 * LANES), 1) >= LANES).astype(jnp.int32)

    def step(pair, total):
        for r in range(rows):
            index = jnp.concatenate(
                [idx_ref[2 * pair, r : r + 1, :], idx_ref[2 * pair + 1, r : r + 1, :]], axis=1
            )
            row = ((2 * pair + second) * rows + r).astype(F32)
            here = det_id == index // length
            stacked = [
                jnp.where(here, jnp.broadcast_to(piece, here.shape), 0.0) for piece in (row, lane)
            ]
            total = total + lax.dot_general(
                jnp.concatenate(stacked, axis=0).astype(BF16),
                one_hot_cols(index & (length - 1), length),
                NT,
                preferred_element_type=F32,
            )
        return total

    total = lax.fori_loop(
        0, owners // 2, step, jnp.zeros((2 * det_local, length), F32), unroll=16
    )
    slot_ref[...] = (total[:det_local] * LANES + total[det_local:]).astype(jnp.int32)


def invert(idx, shape):
    return pl.pallas_call(
        invert_kernel,
        out_shape=jax.ShapeDtypeStruct(shape, jnp.int32),
        in_specs=[VMEM_SPEC],
        out_specs=VMEM_SPEC,
        compiler_params=pltpu.CompilerParams(vmem_limit_bytes=VMEM_LIMIT),
        name="invert",
    )(idx)


def residual_kernel(got_ref, slot_ref, clean_ref, out_ref, rows_ref):
    owners, rows = got_ref.shape[0], got_ref.shape[1]
    for o in range(owners):
        rows_ref[o * rows : (o + 1) * rows, :] = got_ref[o]
    parts = jnp.concatenate(split2(rows_ref[...]), axis=0).astype(BF16)
    depth = owners * rows
    row_id = iota((depth, slot_ref.shape[1]), 0)
    for d in range(slot_ref.shape[0]):
        slot = slot_ref[d : d + 1, :]
        found = lax.dot_general(
            parts, one_hot_cols(slot & (LANES - 1), LANES), NN, preferred_element_type=F32
        )
        here = jnp.where(row_id == slot >> 7, found[:depth] + found[depth:], 0.0)
        out_ref[d : d + 1, :] = clean_ref[d : d + 1, :] - jnp.sum(here, axis=0, keepdims=True)


def residuals(got, slot, cleaned):
    return pl.pallas_call(
        residual_kernel,
        out_shape=jax.ShapeDtypeStruct(cleaned.shape, F32),
        in_specs=[VMEM_SPEC] * 3,
        out_specs=VMEM_SPEC,
        scratch_shapes=[pltpu.VMEM((got.shape[0] * got.shape[1], LANES), F32)],
        compiler_params=pltpu.CompilerParams(vmem_limit_bytes=VMEM_LIMIT),
        name="residuals",
    )(got, slot, cleaned)


def shards(timestream, tile_index, pixel_index, angle_bin, owner_map):
    blocks, det_local, sample_local = timestream.shape
    samples = timestream[0]
    tm_count = lax.axis_size("tm")
    det_count = lax.axis_size("det")
    owners = tm_count * det_count
    flat = det_local * sample_local
    rows = flat // (owners // 2) // LANES

    parts = [samples] + [
        lax.ppermute(samples, "det", [(i, (i + k) % det_count) for i in range(det_count)])
        for k in range(1, det_count)
    ]
    def flatten(x):
        x = x.reshape(det_local // 8, 8, sample_local // LANES, LANES)
        return x.transpose(0, 2, 1, 3).reshape(flat)

    number = jnp.arange(flat, dtype=jnp.int32).reshape(tile_index.shape)
    key = flatten((tile_index << PIX_BITS) + pixel_index)
    load = flatten((number << 10) + angle_bin)
    key, load = lax.sort((key, load), num_keys=1, is_stable=False)
    key, load, parts = lax.optimization_barrier((key, load, parts))
    templates, products = modes(parts, det_local * det_count // MODES)
    key, load, products = lax.optimization_barrier((key, load, products))
    send, idx = route(key, load, owner_map, owners, rows)
    products = products + lax.ppermute(products, "tm", [(i, i ^ 1) for i in range(tm_count)])
    products, send = lax.optimization_barrier((products, send))
    products = [products] + [
        lax.ppermute(products, "tm", [(i, (i + k) % tm_count) for i in range(tm_count)])
        for k in range(2, tm_count, 2)
    ]
    everywhere = functools.partial(
        lax.all_to_all, axis_name=("tm", "det"), split_axis=0, concat_axis=0, tiled=True
    )
    got = everywhere(send)
    cleaned, pay = clean(products, templates, samples, idx)
    mixed, acc = angles(got, rows)

    values = everywhere(pay)
    sky, back = make_map(values, mixed, acc)
    residual = residuals(everywhere(back), invert(idx, samples.shape), cleaned)
    return (sky, residual.reshape(blocks, det_local, sample_local))


def solution(mesh):
    placed = (
        P("tm", "det", None),
        P("tm", "det", None),
        P("tm", "det", None),
        P("tm", "det", None),
        P(),
    )
    return jax.shard_map(
        shards,
        mesh=mesh,
        in_specs=placed,
        out_specs=(P(None, ("tm", "det")), P("tm", "det", None)),
        check_vma=False,
    )
```

```python
import functools

import jax
import jax.numpy as jnp
from jax import lax
from jax.experimental import pallas as pl
from jax.experimental.pallas import tpu as pltpu
from jax.sharding import PartitionSpec as P

MODES = 16
NBINS = 1024
TILE_PIX = 32640
RIDGE = 1.0
LANES = 128
LO = 256
HI = -(-TILE_PIX // LO)
WIN = 32
HIP = HI + WIN - 8
SUB = 32
WAYS = LANES // SUB
GROUP = 8
PIX_BITS = 15
HALF = LANES // 2
F32 = jnp.float32
BF16 = jnp.bfloat16
HIGHEST = lax.Precision.HIGHEST
NT = (((1,), (1,)), ((), ()))
NN = (((1,), (0,)), ((), ()))
VMEM_LIMIT = 24 * 1024 * 1024
VMEM_SPEC = pl.BlockSpec(memory_space=pltpu.VMEM)


def iota(shape, dim):
    return lax.broadcasted_iota(jnp.int32, shape, dim)


def split3(x):
    first = x.astype(BF16).astype(F32)
    rest = x - first
    second = rest.astype(BF16).astype(F32)
    return first, second, rest - second


def split2(x):
    return split3(x)[:2]


def one_hot_cols(row, rows):
    ids = iota((rows, row.shape[1]), 0).astype(F32).astype(BF16)
    want = jnp.broadcast_to(row.astype(F32).astype(BF16), ids.shape)
    return jnp.where(ids == want, jnp.ones_like(ids), jnp.zeros_like(ids))


def modes_kernel(members, *refs):
    part_refs = refs[:-2]
    temp_ref, out_ref = refs[-2:]
    own_ref = part_refs[0]
    groups = own_ref.shape[0] // MODES
    templates = sum(ref[g * MODES : (g + 1) * MODES, :] for ref in part_refs for g in range(groups))
    templates = templates / members
    temp_ref[...] = templates
    both = jnp.concatenate([templates, own_ref[...]], axis=0)
    products = lax.dot_general(templates, both, NT, precision=HIGHEST, preferred_element_type=F32)
    pad = jnp.zeros((MODES, HALF - products.shape[1]), F32)
    half = jnp.concatenate([products, pad], axis=1)
    out_ref[...] = jnp.concatenate([half[: MODES // 2], half[MODES // 2 :]], axis=1)


def modes(parts, members):
    return pl.pallas_call(
        functools.partial(modes_kernel, members),
        out_shape=(
            jax.ShapeDtypeStruct((MODES, parts[0].shape[1]), F32),
            jax.ShapeDtypeStruct((MODES // 2, LANES), F32),
        ),
        in_specs=[VMEM_SPEC] * len(parts),
        out_specs=(VMEM_SPEC, VMEM_SPEC),
        compiler_params=pltpu.CompilerParams(vmem_limit_bytes=VMEM_LIMIT),
        name="modes",
    )(*parts)


def route_kernel(owner_ref, key_ref, load_ref, send_ref, idx_ref, keys, loads):
    tiles, rows = idx_ref.shape[0], idx_ref.shape[1]
    depth = key_ref.shape[0]
    keys[0:depth, :] = key_ref[...]
    loads[0:depth, :] = load_ref[...]
    keys[depth:, :] = jnp.zeros((8, LANES), jnp.int32)
    loads[depth:, :] = jnp.zeros((8, LANES), jnp.int32)
    sorted_keys = key_ref[...]
    lane = iota((8, LANES), 1)
    slot = iota((8, LANES), 0) * LANES + lane
    starts = [jnp.int32(0)]
    for tile in range(1, tiles):
        below = (sorted_keys < (tile << PIX_BITS)).astype(F32)
        starts.append(jnp.sum(below).astype(jnp.int32))
    starts.append(jnp.int32(depth * LANES))
    for tile in range(tiles):
        start = starts[tile]
        count = starts[tile + 1] - start
        top = start // LANES
        shift = start % LANES
        back = lax.rem(LANES - shift, LANES)
        whole = lane < LANES - shift

        def run(ref):
            turned = pltpu.roll(ref[pl.ds(top, 8), :], back, 1)
            return jnp.where(whole, turned, pltpu.roll(turned, 7, 0))

        key = run(keys)
        load = run(loads)
        live = slot < count
        owner = owner_ref[tile]
        pixel = jnp.where(live, key & ((1 << PIX_BITS) - 1), -1)
        index = jnp.where(live, load >> 10, -1)
        send_ref[owner, 0:rows, :] = pixel[0:rows]
        send_ref[owner, rows : 2 * rows, :] = (load & (NBINS - 1))[0:rows]
        idx_ref[owner, :, :] = index[0:rows]


def route(key, load, owner_map, owners, rows):
    flat = key.shape[0]
    depth = flat // LANES
    return pl.pallas_call(
        route_kernel,
        out_shape=(
            jax.ShapeDtypeStruct((owners, 2 * rows, LANES), jnp.int32),
            jax.ShapeDtypeStruct((owners, rows, LANES), jnp.int32),
        ),
        in_specs=[pl.BlockSpec(memory_space=pltpu.SMEM), VMEM_SPEC, VMEM_SPEC],
        out_specs=(VMEM_SPEC, VMEM_SPEC),
        scratch_shapes=[
            pltpu.VMEM((depth + 8, LANES), jnp.int32),
            pltpu.VMEM((depth + 8, LANES), jnp.int32),
        ],
        compiler_params=pltpu.CompilerParams(vmem_limit_bytes=VMEM_LIMIT),
        name="route",
    )(owner_map, key.reshape(depth, LANES), load.reshape(depth, LANES))


def pair_row(ref, pair, r):
    return jnp.concatenate([ref[2 * pair, r : r + 1, :], ref[2 * pair + 1, r : r + 1, :]], axis=1)


def pick_kernel(temp_ref, samples_ref, idx_ref, raw_ref, there_ref):
    det_local, length = samples_ref.shape
    owners, rows = idx_ref.shape[0], idx_ref.shape[1]
    terms = split3(samples_ref[...]) + split3(temp_ref[...])
    parts = jnp.concatenate(terms, axis=0).astype(BF16)
    det_id = iota((det_local, 2 * LANES), 0)

    def step(pair, _):
        for r in range(rows):
            index = pair_row(idx_ref, pair, r)
            found = lax.dot_general(
                parts, one_hot_cols(index & (length - 1), length), NN, preferred_element_type=F32
            )
            own = sum(found[i * det_local : (i + 1) * det_local] for i in range(3))
            here = jnp.where(det_id == index // length, own, 0.0)
            value = jnp.sum(here, axis=0, keepdims=True)
            raw_ref[2 * pair, r : r + 1, :] = value[:, :LANES]
            raw_ref[2 * pair + 1, r : r + 1, :] = value[:, LANES:]
            found = found[3 * det_local :]
            there_ref[pair, r] = sum(found[i * MODES : (i + 1) * MODES] for i in range(3))
        return 0

    lax.fori_loop(0, owners // 2, step, 0, unroll=16)


def pick(templates, samples, idx):
    owners, rows = idx.shape[:2]
    return pl.pallas_call(
        pick_kernel,
        out_shape=(
            jax.ShapeDtypeStruct(idx.shape, F32),
            jax.ShapeDtypeStruct((owners // 2, rows, MODES, 2 * LANES), F32),
        ),
        in_specs=[VMEM_SPEC] * 3,
        out_specs=(VMEM_SPEC, VMEM_SPEC),
        compiler_params=pltpu.CompilerParams(vmem_limit_bytes=VMEM_LIMIT),
        name="pick",
    )(templates, samples, idx)


def clean_kernel(length, raw_ref, there_ref, idx_ref, *refs):
    coef_ref, pay_ref = refs[-2:]
    det_local = coef_ref.shape[1]
    owners, rows = idx_ref.shape[0], idx_ref.shape[1]
    packed = sum(ref[...] for ref in refs[:-2])
    system = jnp.concatenate([packed, pltpu.roll(packed, HALF, 1)], axis=0)
    row_id = iota((MODES, LANES), 0)
    lane_id = iota((MODES, LANES), 1)
    system = system + jnp.where(row_id == lane_id, RIDGE, 0.0)
    for k in range(MODES):
        pivot = system[k : k + 1, :] / system[k : k + 1, k : k + 1]
        column = system[:, k : k + 1]
        system = jnp.where(row_id == k, pivot, system - column * pivot)
    coef = system[:, MODES : MODES + det_local]
    coef_ref[...] = coef
    parts = jnp.concatenate(split3(coef), axis=0).astype(BF16)

    def step(pair, _):
        for r in range(rows):
            index = pair_row(idx_ref, pair, r)
            found = lax.dot_general(
                parts,
                one_hot_cols(jnp.where(index < 0, det_local, index // length), det_local),
                NN,
                preferred_element_type=F32,
            )
            weight = sum(found[i * MODES : (i + 1) * MODES] for i in range(3))
            model = jnp.sum(weight * there_ref[pair, r], axis=0, keepdims=True)
            value = pair_row(raw_ref, pair, r) - model
            pay_ref[2 * pair, r : r + 1, :] = value[:, :LANES]
            pay_ref[2 * pair + 1, r : r + 1, :] = value[:, LANES:]
        return 0

    lax.fori_loop(0, owners // 2, step, 0, unroll=16)


def clean(sums, raw, there, idx, shape):
    det_local, length = shape
    return pl.pallas_call(
        functools.partial(clean_kernel, length),
        out_shape=(
            jax.ShapeDtypeStruct((MODES, det_local), F32),
            jax.ShapeDtypeStruct(idx.shape, F32),
        ),
        in_specs=[VMEM_SPEC] * (3 + len(sums)),
        out_specs=(VMEM_SPEC, VMEM_SPEC),
        compiler_params=pltpu.CompilerParams(vmem_limit_bytes=VMEM_LIMIT),
        name="clean",
    )(raw, there, idx, *sums)


def shuffle(blocks, lane):
    blocks = list(blocks)
    width = HALF
    while width >= SUB:
        low = (lane & width) == 0
        step = width // SUB
        for i in range(WAYS):
            if i & step == 0:
                a, b = blocks[i], blocks[i + step]
                blocks[i] = jnp.where(low, a, pltpu.roll(b, width, 1))
                blocks[i + step] = jnp.where(low, pltpu.roll(a, LANES - width, 1), b)
        width //= 2
    return blocks


def chunk_row(ref, run, group, r):
    return jnp.concatenate([ref[run, GROUP * group + i, r : r + 1, :] for i in range(GROUP)], axis=1)


def over_chunks(groups, rows, table_ref, body):
    def step(i, _):
        run, group = lax.rem(i, WAYS), lax.div(i, WAYS)
        ends = [(table_ref[r, 2 * i], table_ref[r, 2 * i + 1]) for r in range(rows)]
        widest = functools.reduce(jnp.maximum, [high - low for low, high in ends])

        for r in range(rows):
            body(run, group, r, ends[r][0], True)

        @pl.when(widest >= WIN // 8)
        def _():
            for r in range(rows):
                low, high = ends[r]

                def more(w, _):
                    body(run, group, r, low + w * (WIN // 8), False)
                    return 0

                lax.fori_loop(1, (high - low) // (WIN // 8) + 1, more, 0)

        return 0

    lax.fori_loop(0, groups * WAYS, step, 0)


def windows_of(pix_ref, groups, rows):
    table_lane = iota((rows, LANES), 1)
    windows = jnp.zeros((rows, LANES), jnp.int32)
    for group in range(groups):
        for run in range(WAYS):
            ends = [pix_ref[run, group * GROUP + i] for i in range(GROUP)]
            most = functools.reduce(jnp.maximum, ends)
            least = functools.reduce(
                jnp.minimum, [jnp.where(x < 0, TILE_PIX - 1, x) for x in ends]
            )
            most = jnp.max(most, axis=1, keepdims=True)
            least = jnp.min(least, axis=1, keepdims=True)
            high = most >> 11
            low = jnp.where(most < 0, 0, least >> 11)
            at = 2 * (group * WAYS + run)
            windows = jnp.where(table_lane == at, low, windows)
            windows = jnp.where(table_lane == at + 1, high, windows)
    return windows


def scatter_add(sum_ref, terms, pieces, pixel, first):
    start = pl.multiple_of(first * 8, 8)
    here = (iota((WIN, pixel.shape[1]), 0) + start) == (pixel >> 8)
    stacked = [jnp.where(here, jnp.broadcast_to(x, here.shape), 0.0) for x in pieces]
    found = lax.dot_general(
        jnp.concatenate(stacked, axis=0).astype(BF16),
        one_hot_cols(pixel & (LO - 1), LO),
        NT,
        preferred_element_type=F32,
    )
    at = 0
    for q, count in enumerate(terms):
        total = found[at : at + WIN]
        for i in range(1, count):
            total = total + found[at + i * WIN : at + (i + 1) * WIN]
        at += count * WIN
        sum_ref[q, pl.ds(start, WIN), :] += total


ANGLE_TERMS = (1, 3, 3, 3, 3)
VALUE_TERMS = (2, 3, 3)


def angles_kernel(got_ref, mixed_ref, sum_ref, pix_ref, parts_ref, table_vmem, table, sem):
    owners, rows = got_ref.shape[0], mixed_ref.shape[3]
    groups = owners // WAYS // GROUP
    lane = iota((2 * rows, LANES), 1)
    for at in range(owners // WAYS):
        mixed = shuffle([got_ref[at * WAYS + i] for i in range(WAYS)], lane)
        for run in range(WAYS):
            pix_ref[run, at] = mixed[run][:rows]
            mixed_ref[0, run, at] = mixed[run][:rows].astype(F32)
    table_vmem[...] = windows_of(pix_ref, groups, rows)
    copy = pltpu.make_async_copy(table_vmem, table, sem)
    copy.start()
    for at in range(owners // WAYS):
        mixed = shuffle([got_ref[at * WAYS + i] for i in range(WAYS)], lane)
        for run in range(WAYS):
            angle = (jnp.pi * mixed[run][rows:].astype(F32) / NBINS) * 2.0
            cosine, sine = jnp.cos(angle), jnp.sin(angle)
            mixed_ref[1, run, at] = cosine
            mixed_ref[2, run, at] = sine
            parts = (
                split3(cosine) + split3(sine) + split3(cosine * cosine) + split3(cosine * sine)
            )
            for p, part in enumerate(parts):
                parts_ref[p, run, at] = part
    sum_ref[...] = jnp.zeros_like(sum_ref)
    copy.wait()

    def add(run, group, r, first, _):
        pixel = chunk_row(pix_ref, run, group, r)
        pieces = [jnp.ones(pixel.shape, F32)]
        pieces += [chunk_row(parts_ref.at[p], run, group, r) for p in range(parts_ref.shape[0])]
        scatter_add(sum_ref, ANGLE_TERMS, pieces, pixel, first)

    over_chunks(groups, rows, table, add)


def angles(got, rows):
    mixed = (WAYS, got.shape[0] // WAYS, rows, LANES)
    return pl.pallas_call(
        angles_kernel,
        out_shape=(
            jax.ShapeDtypeStruct((3,) + mixed, F32),
            jax.ShapeDtypeStruct((len(ANGLE_TERMS), HIP, LO), F32),
        ),
        in_specs=[VMEM_SPEC],
        out_specs=(VMEM_SPEC, VMEM_SPEC),
        scratch_shapes=[
            pltpu.VMEM(mixed, jnp.int32),
            pltpu.VMEM((sum(ANGLE_TERMS) - 1,) + mixed, F32),
            pltpu.VMEM((rows, LANES), jnp.int32),
            pltpu.SMEM((rows, LANES), jnp.int32),
            pltpu.SemaphoreType.DMA,
        ],
        compiler_params=pltpu.CompilerParams(vmem_limit_bytes=VMEM_LIMIT),
        name="angles",
    )(got)


def solve_stokes(sums):
    a11 = sums[0] + RIDGE
    a12 = sums[1]
    a13 = sums[2]
    a22 = sums[3] + RIDGE
    a23 = sums[4]
    a33 = sums[5] + RIDGE
    c11 = a22 * a33 - a23 * a23
    c12 = a13 * a23 - a12 * a33
    c13 = a12 * a23 - a13 * a22
    c22 = a11 * a33 - a13 * a13
    c23 = a12 * a13 - a11 * a23
    c33 = a11 * a22 - a12 * a12
    inverse = 1.0 / (a11 * c11 + a12 * c12 + a13 * c13)
    stokes_i = (c11 * sums[6] + c12 * sums[7] + c13 * sums[8]) * inverse
    stokes_q = (c12 * sums[6] + c22 * sums[7] + c23 * sums[8]) * inverse
    stokes_u = (c13 * sums[6] + c23 * sums[7] + c33 * sums[8]) * inverse
    return (stokes_i, stokes_q, stokes_u)


def map_kernel(
    got_ref, mixed_ref, acc_ref, sky_ref, back_ref, pix_ref, parts_ref, sum_ref, table_vmem, table, sem
):
    owners, rows = got_ref.shape[0], got_ref.shape[1]
    groups = owners // WAYS // GROUP
    lane = iota((rows, LANES), 1)
    cos_ref, sin_ref = mixed_ref.at[1], mixed_ref.at[2]
    pix_ref[...] = mixed_ref[0].astype(jnp.int32)
    table_vmem[...] = windows_of(pix_ref, groups, rows)
    copy = pltpu.make_async_copy(table_vmem, table, sem)
    copy.start()
    for at in range(owners // WAYS):
        mixed = shuffle([got_ref[at * WAYS + i] for i in range(WAYS)], lane)
        for run in range(WAYS):
            value, cosine, sine = mixed[run], cos_ref[run, at], sin_ref[run, at]
            parts = split2(value) + split3(cosine * value) + split3(sine * value)
            for p, part in enumerate(parts):
                parts_ref[p, run, at] = part
    sum_ref[...] = jnp.zeros_like(sum_ref)
    copy.wait()

    def add(run, group, r, first, _):
        pixel = chunk_row(pix_ref, run, group, r)
        pieces = [chunk_row(parts_ref.at[p], run, group, r) for p in range(parts_ref.shape[0])]
        scatter_add(sum_ref, VALUE_TERMS, pieces, pixel, first)

    over_chunks(groups, rows, table, add)

    for block in range(HI // 8):
        at = pl.ds(block * 8, 8)
        sums = [acc_ref[q, at, :] for q in range(5)]
        sums += [sums[0] - sums[3]] + [sum_ref[q, at, :] for q in range(3)]
        stokes = solve_stokes(sums)
        for q in range(3):
            sum_ref[q, at, :] = stokes[q]
            for i in range(8):
                first = (block * 8 + i) * LO
                width = min(LO, TILE_PIX - first)
                sky_ref[q : q + 1, first : first + width] = stokes[q][i : i + 1, :width]

    def look(run, group, r, first, fresh):
        pixel = chunk_row(pix_ref, run, group, r)
        start = pl.multiple_of(first * 8, 8)
        planes = [x for q in range(3) for x in split2(sum_ref[q, pl.ds(start, WIN), :])]
        found = lax.dot_general(
            jnp.concatenate(planes, axis=0).astype(BF16),
            one_hot_cols(pixel & (LO - 1), LO),
            NN,
            preferred_element_type=F32,
        )
        stokes = [
            found[2 * q * WIN : (2 * q + 1) * WIN] + found[(2 * q + 1) * WIN : (2 * q + 2) * WIN]
            for q in range(3)
        ]
        cosine = chunk_row(cos_ref, run, group, r)
        sine = chunk_row(sin_ref, run, group, r)
        signal = stokes[0] + cosine * stokes[1] + sine * stokes[2]
        here = (iota(signal.shape, 0) + start) == (pixel >> 8)
        value = jnp.sum(jnp.where(here, signal, 0.0), axis=0, keepdims=True)
        for i in range(GROUP):
            part = value[:, i * LANES : (i + 1) * LANES]
            if fresh:
                parts_ref[0, run, GROUP * group + i, r : r + 1, :] = part
            else:
                parts_ref[0, run, GROUP * group + i, r : r + 1, :] += part

    over_chunks(groups, rows, table, look)

    for at in range(owners // WAYS):
        mixed = shuffle([parts_ref[0, run, at] for run in range(WAYS)], lane)
        for i in range(WAYS):
            back_ref[at * WAYS + i] = mixed[i]


def make_map(got, mixed, acc):
    rows = got.shape[1]
    return pl.pallas_call(
        map_kernel,
        out_shape=(
            jax.ShapeDtypeStruct((3, TILE_PIX), F32),
            jax.ShapeDtypeStruct(got.shape, F32),
        ),
        in_specs=[VMEM_SPEC] * 3,
        out_specs=(VMEM_SPEC, VMEM_SPEC),
        scratch_shapes=[
            pltpu.VMEM(mixed.shape[1:], jnp.int32),
            pltpu.VMEM((sum(VALUE_TERMS),) + mixed.shape[1:], F32),
            pltpu.VMEM((len(VALUE_TERMS), HIP, LO), F32),
            pltpu.VMEM((rows, LANES), jnp.int32),
            pltpu.SMEM((rows, LANES), jnp.int32),
            pltpu.SemaphoreType.DMA,
        ],
        compiler_params=pltpu.CompilerParams(vmem_limit_bytes=VMEM_LIMIT),
        name="make_map",
    )(got, mixed, acc)


def invert_kernel(idx_ref, coef_ref, temp_ref, samples_ref, slot_ref, clean_ref):
    det_local, length = slot_ref.shape
    clean_ref[...] = samples_ref[...] - lax.dot_general(
        coef_ref[...],
        temp_ref[...],
        (((0,), (0,)), ((), ())),
        precision=HIGHEST,
        preferred_element_type=F32,
    )
    owners, rows = idx_ref.shape[0], idx_ref.shape[1]
    det_id = iota((det_local, 2 * LANES), 0)
    lane = lax.rem(iota((1, 2 * LANES), 1), LANES).astype(F32)
    second = (iota((1, 2 * LANES), 1) >= LANES).astype(jnp.int32)

    def step(pair, total):
        for r in range(rows):
            index = jnp.concatenate(
                [idx_ref[2 * pair, r : r + 1, :], idx_ref[2 * pair + 1, r : r + 1, :]], axis=1
            )
            row = ((2 * pair + second) * rows + r).astype(F32)
            here = det_id == index // length
            stacked = [
                jnp.where(here, jnp.broadcast_to(piece, here.shape), 0.0) for piece in (row, lane)
            ]
            total = total + lax.dot_general(
                jnp.concatenate(stacked, axis=0).astype(BF16),
                one_hot_cols(index & (length - 1), length),
                NT,
                preferred_element_type=F32,
            )
        return total

    total = lax.fori_loop(
        0, owners // 2, step, jnp.zeros((2 * det_local, length), F32), unroll=16
    )
    slot_ref[...] = (total[:det_local] * LANES + total[det_local:]).astype(jnp.int32)


def invert(idx, coef, templates, samples):
    return pl.pallas_call(
        invert_kernel,
        out_shape=(
            jax.ShapeDtypeStruct(samples.shape, jnp.int32),
            jax.ShapeDtypeStruct(samples.shape, F32),
        ),
        in_specs=[VMEM_SPEC] * 4,
        out_specs=(VMEM_SPEC, VMEM_SPEC),
        compiler_params=pltpu.CompilerParams(vmem_limit_bytes=VMEM_LIMIT),
        name="invert",
    )(idx, coef, templates, samples)


def residual_kernel(got_ref, slot_ref, clean_ref, out_ref, rows_ref):
    owners, rows = got_ref.shape[0], got_ref.shape[1]
    for o in range(owners):
        rows_ref[o * rows : (o + 1) * rows, :] = got_ref[o]
    parts = jnp.concatenate(split2(rows_ref[...]), axis=0).astype(BF16)
    depth = owners * rows
    row_id = iota((depth, slot_ref.shape[1]), 0)
    for d in range(slot_ref.shape[0]):
        slot = slot_ref[d : d + 1, :]
        found = lax.dot_general(
            parts, one_hot_cols(slot & (LANES - 1), LANES), NN, preferred_element_type=F32
        )
        here = jnp.where(row_id == slot >> 7, found[:depth] + found[depth:], 0.0)
        out_ref[d : d + 1, :] = clean_ref[d : d + 1, :] - jnp.sum(here, axis=0, keepdims=True)


def residuals(got, slot, cleaned):
    return pl.pallas_call(
        residual_kernel,
        out_shape=jax.ShapeDtypeStruct(cleaned.shape, F32),
        in_specs=[VMEM_SPEC] * 3,
        out_specs=VMEM_SPEC,
        scratch_shapes=[pltpu.VMEM((got.shape[0] * got.shape[1], LANES), F32)],
        compiler_params=pltpu.CompilerParams(vmem_limit_bytes=VMEM_LIMIT),
        name="residuals",
    )(got, slot, cleaned)


def shards(timestream, tile_index, pixel_index, angle_bin, owner_map):
    blocks, det_local, sample_local = timestream.shape
    samples = timestream[0]
    tm_count = lax.axis_size("tm")
    det_count = lax.axis_size("det")
    owners = tm_count * det_count
    flat = det_local * sample_local
    rows = flat // (owners // 2) // LANES

    parts = [samples] + [
        lax.ppermute(samples, "det", [(i, (i + k) % det_count) for i in range(det_count)])
        for k in range(1, det_count)
    ]
    def flatten(x):
        x = x.reshape(det_local // 8, 8, sample_local // LANES, LANES)
        return x.transpose(0, 2, 1, 3).reshape(flat)

    number = jnp.arange(flat, dtype=jnp.int32).reshape(tile_index.shape)
    key = flatten((tile_index << PIX_BITS) + pixel_index)
    load = flatten((number << 10) + angle_bin)
    templates, products = modes(parts, det_local * det_count // MODES)

    def partners(x, bit):
        return lax.ppermute(x, "tm", [(i, i ^ bit) for i in range(tm_count)])

    key, load, products = lax.optimization_barrier((key, load, products))
    found = partners(products, 1)
    key, load = lax.sort((key, load), num_keys=1, is_stable=False)
    key, load, found = lax.optimization_barrier((key, load, found))
    products = products + found
    found = partners(products, 2)
    send, idx = route(key, load, owner_map, owners, rows)
    send, found = lax.optimization_barrier((send, found))
    products = products + found
    bit = 4
    while bit < tm_count:
        found = partners(products, bit)
        bit *= 2
        if bit < tm_count:
            products = products + found
    products = [products, found]
    everywhere = functools.partial(
        lax.all_to_all, axis_name=("tm", "det"), split_axis=0, concat_axis=0, tiled=True
    )
    got = everywhere(send)
    raw, there = pick(templates, samples, idx)
    coef, pay = clean(products, raw, there, idx, samples.shape)
    mixed, acc = angles(got, rows)

    values = everywhere(pay)
    sky, back = make_map(values, mixed, acc)
    slot, cleaned = invert(idx, coef, templates, samples)
    residual = residuals(everywhere(back), slot, cleaned)
    return (sky, residual.reshape(blocks, det_local, sample_local))


def solution(mesh):
    placed = (
        P("tm", "det", None),
        P("tm", "det", None),
        P("tm", "det", None),
        P("tm", "det", None),
        P(),
    )
    return jax.shard_map(
        shards,
        mesh=mesh,
        in_specs=placed,
        out_specs=(P(None, ("tm", "det")), P("tm", "det", None)),
        check_vma=False,
    )
```

```python
import functools

import jax
import jax.numpy as jnp
from jax import lax
from jax.experimental import pallas as pl
from jax.experimental.pallas import tpu as pltpu
from jax.sharding import PartitionSpec as P

MODES = 16
NBINS = 1024
TILE_PIX = 32640
RIDGE = 1.0
LANES = 128
LO = 256
HI = -(-TILE_PIX // LO)
WIN = 32
HIP = HI + WIN - 8
SUB = 32
WAYS = LANES // SUB
GROUP = 8
PIX_BITS = 15
HALF = LANES // 2
F32 = jnp.float32
BF16 = jnp.bfloat16
HIGHEST = lax.Precision.HIGHEST
NT = (((1,), (1,)), ((), ()))
NN = (((1,), (0,)), ((), ()))
VMEM_LIMIT = 24 * 1024 * 1024
VMEM_SPEC = pl.BlockSpec(memory_space=pltpu.VMEM)


def iota(shape, dim):
    return lax.broadcasted_iota(jnp.int32, shape, dim)


def split3(x):
    first = x.astype(BF16).astype(F32)
    rest = x - first
    second = rest.astype(BF16).astype(F32)
    return first, second, rest - second


def split2(x):
    return split3(x)[:2]


def one_hot_cols(row, rows):
    ids = iota((rows, row.shape[1]), 0).astype(F32).astype(BF16)
    want = jnp.broadcast_to(row.astype(F32).astype(BF16), ids.shape)
    return jnp.where(ids == want, jnp.ones_like(ids), jnp.zeros_like(ids))


def modes_kernel(members, *refs):
    part_refs = refs[:-2]
    temp_ref, out_ref = refs[-2:]
    own_ref = part_refs[0]
    groups = own_ref.shape[0] // MODES
    templates = sum(ref[g * MODES : (g + 1) * MODES, :] for ref in part_refs for g in range(groups))
    templates = templates / members
    temp_ref[...] = templates
    both = jnp.concatenate([templates, own_ref[...]], axis=0)
    products = lax.dot_general(templates, both, NT, precision=HIGHEST, preferred_element_type=F32)
    pad = jnp.zeros((MODES, HALF - products.shape[1]), F32)
    half = jnp.concatenate([products, pad], axis=1)
    out_ref[...] = jnp.concatenate([half[: MODES // 2], half[MODES // 2 :]], axis=1)


def modes(parts, members):
    return pl.pallas_call(
        functools.partial(modes_kernel, members),
        out_shape=(
            jax.ShapeDtypeStruct((MODES, parts[0].shape[1]), F32),
            jax.ShapeDtypeStruct((MODES // 2, LANES), F32),
        ),
        in_specs=[VMEM_SPEC] * len(parts),
        out_specs=(VMEM_SPEC, VMEM_SPEC),
        compiler_params=pltpu.CompilerParams(vmem_limit_bytes=VMEM_LIMIT),
        name="modes",
    )(*parts)


def route_kernel(owner_ref, key_ref, load_ref, send_ref, idx_ref, keys, loads):
    tiles, rows = idx_ref.shape[0], idx_ref.shape[1]
    depth = key_ref.shape[0]
    keys[0:depth, :] = key_ref[...]
    loads[0:depth, :] = load_ref[...]
    keys[depth:, :] = jnp.zeros((8, LANES), jnp.int32)
    loads[depth:, :] = jnp.zeros((8, LANES), jnp.int32)
    sorted_keys = key_ref[...]
    lane = iota((8, LANES), 1)
    slot = iota((8, LANES), 0) * LANES + lane
    starts = [jnp.int32(0)]
    for tile in range(1, tiles):
        below = (sorted_keys < (tile << PIX_BITS)).astype(F32)
        starts.append(jnp.sum(below).astype(jnp.int32))
    starts.append(jnp.int32(depth * LANES))
    for tile in range(tiles):
        start = starts[tile]
        count = starts[tile + 1] - start
        top = start // LANES
        shift = start % LANES
        back = lax.rem(LANES - shift, LANES)
        whole = lane < LANES - shift

        def run(ref):
            turned = pltpu.roll(ref[pl.ds(top, 8), :], back, 1)
            return jnp.where(whole, turned, pltpu.roll(turned, 7, 0))

        key = run(keys)
        load = run(loads)
        live = slot < count
        owner = owner_ref[tile]
        pixel = jnp.where(live, key & ((1 << PIX_BITS) - 1), -1)
        index = jnp.where(live, load >> 10, -1)
        send_ref[owner, 0:rows, :] = pixel[0:rows]
        send_ref[owner, rows : 2 * rows, :] = (load & (NBINS - 1))[0:rows]
        idx_ref[owner, :, :] = index[0:rows]


def route(key, load, owner_map, owners, rows):
    flat = key.shape[0]
    depth = flat // LANES
    return pl.pallas_call(
        route_kernel,
        out_shape=(
            jax.ShapeDtypeStruct((owners, 2 * rows, LANES), jnp.int32),
            jax.ShapeDtypeStruct((owners, rows, LANES), jnp.int32),
        ),
        in_specs=[pl.BlockSpec(memory_space=pltpu.SMEM), VMEM_SPEC, VMEM_SPEC],
        out_specs=(VMEM_SPEC, VMEM_SPEC),
        scratch_shapes=[
            pltpu.VMEM((depth + 8, LANES), jnp.int32),
            pltpu.VMEM((depth + 8, LANES), jnp.int32),
        ],
        compiler_params=pltpu.CompilerParams(vmem_limit_bytes=VMEM_LIMIT),
        name="route",
    )(owner_map, key.reshape(depth, LANES), load.reshape(depth, LANES))


def sky_kernel(stokes_ref, sky_ref):
    for row in range(HI):
        first = row * LO
        width = min(LO, TILE_PIX - first)
        for q in range(3):
            sky_ref[q : q + 1, first : first + width] = stokes_ref[q, row : row + 1, :width]


def lay_out(stokes):
    return pl.pallas_call(
        sky_kernel,
        out_shape=jax.ShapeDtypeStruct((3, TILE_PIX), F32),
        in_specs=[VMEM_SPEC],
        out_specs=VMEM_SPEC,
        compiler_params=pltpu.CompilerParams(vmem_limit_bytes=VMEM_LIMIT),
        name="lay_out",
    )(stokes)


def pair_row(ref, pair, r):
    return jnp.concatenate([ref[2 * pair, r : r + 1, :], ref[2 * pair + 1, r : r + 1, :]], axis=1)


def pick_kernel(temp_ref, samples_ref, idx_ref, raw_ref, there_ref):
    det_local, length = samples_ref.shape
    owners, rows = idx_ref.shape[0], idx_ref.shape[1]
    terms = split3(samples_ref[...]) + split3(temp_ref[...])
    parts = jnp.concatenate(terms, axis=0).astype(BF16)
    det_id = iota((det_local, 2 * LANES), 0)

    def step(pair, _):
        for r in range(rows):
            index = pair_row(idx_ref, pair, r)
            found = lax.dot_general(
                parts, one_hot_cols(index & (length - 1), length), NN, preferred_element_type=F32
            )
            own = sum(found[i * det_local : (i + 1) * det_local] for i in range(3))
            here = jnp.where(det_id == index // length, own, 0.0)
            value = jnp.sum(here, axis=0, keepdims=True)
            raw_ref[2 * pair, r : r + 1, :] = value[:, :LANES]
            raw_ref[2 * pair + 1, r : r + 1, :] = value[:, LANES:]
            found = found[3 * det_local :]
            there_ref[pair, r] = sum(found[i * MODES : (i + 1) * MODES] for i in range(3))
        return 0

    lax.fori_loop(0, owners // 2, step, 0, unroll=16)


def pick(templates, samples, idx):
    owners, rows = idx.shape[:2]
    return pl.pallas_call(
        pick_kernel,
        out_shape=(
            jax.ShapeDtypeStruct(idx.shape, F32),
            jax.ShapeDtypeStruct((owners // 2, rows, MODES, 2 * LANES), F32),
        ),
        in_specs=[VMEM_SPEC] * 3,
        out_specs=(VMEM_SPEC, VMEM_SPEC),
        compiler_params=pltpu.CompilerParams(vmem_limit_bytes=VMEM_LIMIT),
        name="pick",
    )(templates, samples, idx)


def clean_kernel(length, raw_ref, there_ref, idx_ref, *refs):
    coef_ref, pay_ref = refs[-2:]
    det_local = coef_ref.shape[1]
    owners, rows = idx_ref.shape[0], idx_ref.shape[1]
    packed = sum(ref[...] for ref in refs[:-2])
    system = jnp.concatenate([packed, pltpu.roll(packed, HALF, 1)], axis=0)
    row_id = iota((MODES, LANES), 0)
    lane_id = iota((MODES, LANES), 1)
    system = system + jnp.where(row_id == lane_id, RIDGE, 0.0)
    for k in range(MODES):
        pivot = system[k : k + 1, :] / system[k : k + 1, k : k + 1]
        column = system[:, k : k + 1]
        system = jnp.where(row_id == k, pivot, system - column * pivot)
    coef = system[:, MODES : MODES + det_local]
    coef_ref[...] = coef
    parts = jnp.concatenate(split3(coef), axis=0).astype(BF16)

    def step(pair, _):
        for r in range(rows):
            index = pair_row(idx_ref, pair, r)
            found = lax.dot_general(
                parts,
                one_hot_cols(jnp.where(index < 0, det_local, index // length), det_local),
                NN,
                preferred_element_type=F32,
            )
            weight = sum(found[i * MODES : (i + 1) * MODES] for i in range(3))
            model = jnp.sum(weight * there_ref[pair, r], axis=0, keepdims=True)
            value = pair_row(raw_ref, pair, r) - model
            pay_ref[2 * pair, r : r + 1, :] = value[:, :LANES]
            pay_ref[2 * pair + 1, r : r + 1, :] = value[:, LANES:]
        return 0

    lax.fori_loop(0, owners // 2, step, 0, unroll=16)


def clean(sums, raw, there, idx, shape):
    det_local, length = shape
    return pl.pallas_call(
        functools.partial(clean_kernel, length),
        out_shape=(
            jax.ShapeDtypeStruct((MODES, det_local), F32),
            jax.ShapeDtypeStruct(idx.shape, F32),
        ),
        in_specs=[VMEM_SPEC] * (3 + len(sums)),
        out_specs=(VMEM_SPEC, VMEM_SPEC),
        compiler_params=pltpu.CompilerParams(vmem_limit_bytes=VMEM_LIMIT),
        name="clean",
    )(raw, there, idx, *sums)


def shuffle(blocks, lane):
    blocks = list(blocks)
    width = HALF
    while width >= SUB:
        low = (lane & width) == 0
        step = width // SUB
        for i in range(WAYS):
            if i & step == 0:
                a, b = blocks[i], blocks[i + step]
                blocks[i] = jnp.where(low, a, pltpu.roll(b, width, 1))
                blocks[i + step] = jnp.where(low, pltpu.roll(a, LANES - width, 1), b)
        width //= 2
    return blocks


def chunk_row(ref, run, group, r):
    return jnp.concatenate([ref[run, GROUP * group + i, r : r + 1, :] for i in range(GROUP)], axis=1)


def over_chunks(groups, rows, table_ref, body):
    def step(i, _):
        run, group = lax.rem(i, WAYS), lax.div(i, WAYS)
        ends = [(table_ref[r, 2 * i], table_ref[r, 2 * i + 1]) for r in range(rows)]
        widest = functools.reduce(jnp.maximum, [high - low for low, high in ends])

        for r in range(rows):
            body(run, group, r, ends[r][0], True)

        @pl.when(widest >= WIN // 8)
        def _():
            for r in range(rows):
                low, high = ends[r]

                def more(w, _):
                    body(run, group, r, low + w * (WIN // 8), False)
                    return 0

                lax.fori_loop(1, (high - low) // (WIN // 8) + 1, more, 0)

        return 0

    lax.fori_loop(0, groups * WAYS, step, 0)


def windows_of(pix_ref, groups, rows):
    table_lane = iota((rows, LANES), 1)
    windows = jnp.zeros((rows, LANES), jnp.int32)
    for group in range(groups):
        for run in range(WAYS):
            ends = [pix_ref[run, group * GROUP + i] for i in range(GROUP)]
            most = functools.reduce(jnp.maximum, ends)
            least = functools.reduce(
                jnp.minimum, [jnp.where(x < 0, TILE_PIX - 1, x) for x in ends]
            )
            most = jnp.max(most, axis=1, keepdims=True)
            least = jnp.min(least, axis=1, keepdims=True)
            high = most >> 11
            low = jnp.where(most < 0, 0, least >> 11)
            at = 2 * (group * WAYS + run)
            windows = jnp.where(table_lane == at, low, windows)
            windows = jnp.where(table_lane == at + 1, high, windows)
    return windows


def scatter_add(sum_ref, terms, pieces, pixel, first):
    start = pl.multiple_of(first * 8, 8)
    here = (iota((WIN, pixel.shape[1]), 0) + start) == (pixel >> 8)
    stacked = [jnp.where(here, jnp.broadcast_to(x, here.shape), 0.0) for x in pieces]
    found = lax.dot_general(
        jnp.concatenate(stacked, axis=0).astype(BF16),
        one_hot_cols(pixel & (LO - 1), LO),
        NT,
        preferred_element_type=F32,
    )
    at = 0
    for q, count in enumerate(terms):
        total = found[at : at + WIN]
        for i in range(1, count):
            total = total + found[at + i * WIN : at + (i + 1) * WIN]
        at += count * WIN
        sum_ref[q, pl.ds(start, WIN), :] += total


ANGLE_TERMS = (1, 3, 3, 3, 3)
VALUE_TERMS = (2, 3, 3)


def angles_kernel(got_ref, mixed_ref, sum_ref, pix_ref, parts_ref, table_vmem, table, sem):
    owners, rows = got_ref.shape[0], mixed_ref.shape[3]
    groups = owners // WAYS // GROUP
    lane = iota((2 * rows, LANES), 1)
    for at in range(owners // WAYS):
        mixed = shuffle([got_ref[at * WAYS + i] for i in range(WAYS)], lane)
        for run in range(WAYS):
            pix_ref[run, at] = mixed[run][:rows]
            mixed_ref[0, run, at] = mixed[run][:rows].astype(F32)
    table_vmem[...] = windows_of(pix_ref, groups, rows)
    copy = pltpu.make_async_copy(table_vmem, table, sem)
    copy.start()
    for at in range(owners // WAYS):
        mixed = shuffle([got_ref[at * WAYS + i] for i in range(WAYS)], lane)
        for run in range(WAYS):
            angle = (jnp.pi * mixed[run][rows:].astype(F32) / NBINS) * 2.0
            cosine, sine = jnp.cos(angle), jnp.sin(angle)
            mixed_ref[1, run, at] = cosine
            mixed_ref[2, run, at] = sine
            parts = (
                split3(cosine) + split3(sine) + split3(cosine * cosine) + split3(cosine * sine)
            )
            for p, part in enumerate(parts):
                parts_ref[p, run, at] = part
    sum_ref[...] = jnp.zeros_like(sum_ref)
    copy.wait()

    def add(run, group, r, first, _):
        pixel = chunk_row(pix_ref, run, group, r)
        pieces = [jnp.ones(pixel.shape, F32)]
        pieces += [chunk_row(parts_ref.at[p], run, group, r) for p in range(parts_ref.shape[0])]
        scatter_add(sum_ref, ANGLE_TERMS, pieces, pixel, first)

    over_chunks(groups, rows, table, add)


def angles(got, rows):
    mixed = (WAYS, got.shape[0] // WAYS, rows, LANES)
    return pl.pallas_call(
        angles_kernel,
        out_shape=(
            jax.ShapeDtypeStruct((3,) + mixed, F32),
            jax.ShapeDtypeStruct((len(ANGLE_TERMS), HIP, LO), F32),
        ),
        in_specs=[VMEM_SPEC],
        out_specs=(VMEM_SPEC, VMEM_SPEC),
        scratch_shapes=[
            pltpu.VMEM(mixed, jnp.int32),
            pltpu.VMEM((sum(ANGLE_TERMS) - 1,) + mixed, F32),
            pltpu.VMEM((rows, LANES), jnp.int32),
            pltpu.SMEM((rows, LANES), jnp.int32),
            pltpu.SemaphoreType.DMA,
        ],
        compiler_params=pltpu.CompilerParams(vmem_limit_bytes=VMEM_LIMIT),
        name="angles",
    )(got)


def solve_stokes(sums):
    a11 = sums[0] + RIDGE
    a12 = sums[1]
    a13 = sums[2]
    a22 = sums[3] + RIDGE
    a23 = sums[4]
    a33 = sums[5] + RIDGE
    c11 = a22 * a33 - a23 * a23
    c12 = a13 * a23 - a12 * a33
    c13 = a12 * a23 - a13 * a22
    c22 = a11 * a33 - a13 * a13
    c23 = a12 * a13 - a11 * a23
    c33 = a11 * a22 - a12 * a12
    inverse = 1.0 / (a11 * c11 + a12 * c12 + a13 * c13)
    stokes_i = (c11 * sums[6] + c12 * sums[7] + c13 * sums[8]) * inverse
    stokes_q = (c12 * sums[6] + c22 * sums[7] + c23 * sums[8]) * inverse
    stokes_u = (c13 * sums[6] + c23 * sums[7] + c33 * sums[8]) * inverse
    return (stokes_i, stokes_q, stokes_u)


def map_kernel(
    got_ref, mixed_ref, acc_ref, sum_ref, back_ref, pix_ref, parts_ref, table_vmem, table, sem
):
    owners, rows = got_ref.shape[0], got_ref.shape[1]
    groups = owners // WAYS // GROUP
    lane = iota((rows, LANES), 1)
    cos_ref, sin_ref = mixed_ref.at[1], mixed_ref.at[2]
    pix_ref[...] = mixed_ref[0].astype(jnp.int32)
    table_vmem[...] = windows_of(pix_ref, groups, rows)
    copy = pltpu.make_async_copy(table_vmem, table, sem)
    copy.start()
    for at in range(owners // WAYS):
        mixed = shuffle([got_ref[at * WAYS + i] for i in range(WAYS)], lane)
        for run in range(WAYS):
            value, cosine, sine = mixed[run], cos_ref[run, at], sin_ref[run, at]
            parts = split2(value) + split3(cosine * value) + split3(sine * value)
            for p, part in enumerate(parts):
                parts_ref[p, run, at] = part
    sum_ref[...] = jnp.zeros_like(sum_ref)
    copy.wait()

    def add(run, group, r, first, _):
        pixel = chunk_row(pix_ref, run, group, r)
        pieces = [chunk_row(parts_ref.at[p], run, group, r) for p in range(parts_ref.shape[0])]
        scatter_add(sum_ref, VALUE_TERMS, pieces, pixel, first)

    over_chunks(groups, rows, table, add)

    for block in range(HI // 8):
        at = pl.ds(block * 8, 8)
        sums = [acc_ref[q, at, :] for q in range(5)]
        sums += [sums[0] - sums[3]] + [sum_ref[q, at, :] for q in range(3)]
        stokes = solve_stokes(sums)
        for q in range(3):
            sum_ref[q, at, :] = stokes[q]

    def look(run, group, r, first, fresh):
        pixel = chunk_row(pix_ref, run, group, r)
        start = pl.multiple_of(first * 8, 8)
        planes = [x for q in range(3) for x in split2(sum_ref[q, pl.ds(start, WIN), :])]
        found = lax.dot_general(
            jnp.concatenate(planes, axis=0).astype(BF16),
            one_hot_cols(pixel & (LO - 1), LO),
            NN,
            preferred_element_type=F32,
        )
        stokes = [
            found[2 * q * WIN : (2 * q + 1) * WIN] + found[(2 * q + 1) * WIN : (2 * q + 2) * WIN]
            for q in range(3)
        ]
        cosine = chunk_row(cos_ref, run, group, r)
        sine = chunk_row(sin_ref, run, group, r)
        signal = stokes[0] + cosine * stokes[1] + sine * stokes[2]
        here = (iota(signal.shape, 0) + start) == (pixel >> 8)
        value = jnp.sum(jnp.where(here, signal, 0.0), axis=0, keepdims=True)
        for i in range(GROUP):
            part = value[:, i * LANES : (i + 1) * LANES]
            if fresh:
                parts_ref[0, run, GROUP * group + i, r : r + 1, :] = part
            else:
                parts_ref[0, run, GROUP * group + i, r : r + 1, :] += part

    over_chunks(groups, rows, table, look)

    for at in range(owners // WAYS):
        mixed = shuffle([parts_ref[0, run, at] for run in range(WAYS)], lane)
        for i in range(WAYS):
            back_ref[at * WAYS + i] = mixed[i]


def make_map(got, mixed, acc):
    rows = got.shape[1]
    return pl.pallas_call(
        map_kernel,
        out_shape=(
            jax.ShapeDtypeStruct((3, HIP, LO), F32),
            jax.ShapeDtypeStruct(got.shape, F32),
        ),
        in_specs=[VMEM_SPEC] * 3,
        out_specs=(VMEM_SPEC, VMEM_SPEC),
        scratch_shapes=[
            pltpu.VMEM(mixed.shape[1:], jnp.int32),
            pltpu.VMEM((sum(VALUE_TERMS),) + mixed.shape[1:], F32),
            pltpu.VMEM((rows, LANES), jnp.int32),
            pltpu.SMEM((rows, LANES), jnp.int32),
            pltpu.SemaphoreType.DMA,
        ],
        compiler_params=pltpu.CompilerParams(vmem_limit_bytes=VMEM_LIMIT),
        name="make_map",
    )(got, mixed, acc)


def invert_kernel(idx_ref, coef_ref, temp_ref, samples_ref, slot_ref, clean_ref):
    det_local, length = slot_ref.shape
    clean_ref[...] = samples_ref[...] - lax.dot_general(
        coef_ref[...],
        temp_ref[...],
        (((0,), (0,)), ((), ())),
        precision=HIGHEST,
        preferred_element_type=F32,
    )
    owners, rows = idx_ref.shape[0], idx_ref.shape[1]
    det_id = iota((det_local, 2 * LANES), 0)
    lane = lax.rem(iota((1, 2 * LANES), 1), LANES).astype(F32)
    second = (iota((1, 2 * LANES), 1) >= LANES).astype(jnp.int32)

    def step(pair, total):
        for r in range(rows):
            index = jnp.concatenate(
                [idx_ref[2 * pair, r : r + 1, :], idx_ref[2 * pair + 1, r : r + 1, :]], axis=1
            )
            row = ((2 * pair + second) * rows + r).astype(F32)
            here = det_id == index // length
            stacked = [
                jnp.where(here, jnp.broadcast_to(piece, here.shape), 0.0) for piece in (row, lane)
            ]
            total = total + lax.dot_general(
                jnp.concatenate(stacked, axis=0).astype(BF16),
                one_hot_cols(index & (length - 1), length),
                NT,
                preferred_element_type=F32,
            )
        return total

    total = lax.fori_loop(
        0, owners // 2, step, jnp.zeros((2 * det_local, length), F32), unroll=16
    )
    slot_ref[...] = (total[:det_local] * LANES + total[det_local:]).astype(jnp.int32)


def invert(idx, coef, templates, samples):
    return pl.pallas_call(
        invert_kernel,
        out_shape=(
            jax.ShapeDtypeStruct(samples.shape, jnp.int32),
            jax.ShapeDtypeStruct(samples.shape, F32),
        ),
        in_specs=[VMEM_SPEC] * 4,
        out_specs=(VMEM_SPEC, VMEM_SPEC),
        compiler_params=pltpu.CompilerParams(vmem_limit_bytes=VMEM_LIMIT),
        name="invert",
    )(idx, coef, templates, samples)


def residual_kernel(got_ref, slot_ref, clean_ref, out_ref, rows_ref):
    owners, rows = got_ref.shape[0], got_ref.shape[1]
    for o in range(owners):
        rows_ref[o * rows : (o + 1) * rows, :] = got_ref[o]
    parts = jnp.concatenate(split2(rows_ref[...]), axis=0).astype(BF16)
    depth = owners * rows
    row_id = iota((depth, slot_ref.shape[1]), 0)
    for d in range(slot_ref.shape[0]):
        slot = slot_ref[d : d + 1, :]
        found = lax.dot_general(
            parts, one_hot_cols(slot & (LANES - 1), LANES), NN, preferred_element_type=F32
        )
        here = jnp.where(row_id == slot >> 7, found[:depth] + found[depth:], 0.0)
        out_ref[d : d + 1, :] = clean_ref[d : d + 1, :] - jnp.sum(here, axis=0, keepdims=True)


def residuals(got, slot, cleaned):
    return pl.pallas_call(
        residual_kernel,
        out_shape=jax.ShapeDtypeStruct(cleaned.shape, F32),
        in_specs=[VMEM_SPEC] * 3,
        out_specs=VMEM_SPEC,
        scratch_shapes=[pltpu.VMEM((got.shape[0] * got.shape[1], LANES), F32)],
        compiler_params=pltpu.CompilerParams(vmem_limit_bytes=VMEM_LIMIT),
        name="residuals",
    )(got, slot, cleaned)


def shards(timestream, tile_index, pixel_index, angle_bin, owner_map):
    blocks, det_local, sample_local = timestream.shape
    samples = timestream[0]
    tm_count = lax.axis_size("tm")
    det_count = lax.axis_size("det")
    owners = tm_count * det_count
    flat = det_local * sample_local
    rows = flat // (owners // 2) // LANES

    parts = [samples] + [
        lax.ppermute(samples, "det", [(i, (i + k) % det_count) for i in range(det_count)])
        for k in range(1, det_count)
    ]
    def flatten(x):
        x = x.reshape(det_local // 8, 8, sample_local // LANES, LANES)
        return x.transpose(0, 2, 1, 3).reshape(flat)

    number = jnp.arange(flat, dtype=jnp.int32).reshape(tile_index.shape)
    key = flatten((tile_index << PIX_BITS) + pixel_index)
    load = flatten((number << 10) + angle_bin)
    templates, products = modes(parts, det_local * det_count // MODES)

    def partners(x, bit):
        return lax.ppermute(x, "tm", [(i, i ^ bit) for i in range(tm_count)])

    bits = [1 << i for i in reversed(range(tm_count.bit_length() - 1))]
    key, load, products = lax.optimization_barrier((key, load, products))
    found = partners(products, bits[0])
    key, load = lax.sort((key, load), num_keys=1, is_stable=False)
    key, load, found = lax.optimization_barrier((key, load, found))
    products = products + found
    found = partners(products, bits[1])
    send, idx = route(key, load, owner_map, owners, rows)
    send, found = lax.optimization_barrier((send, found))
    for bit in bits[2:]:
        products = products + found
        found = partners(products, bit)
    products = [products, found]
    everywhere = functools.partial(
        lax.all_to_all, axis_name=("tm", "det"), split_axis=0, concat_axis=0, tiled=True
    )
    got = everywhere(send)
    raw, there = pick(templates, samples, idx)
    coef, pay = clean(products, raw, there, idx, samples.shape)
    mixed, acc = angles(got, rows)

    values = everywhere(pay)
    stokes, back = make_map(values, mixed, acc)
    slot, cleaned = invert(idx, coef, templates, samples)
    residual = residuals(everywhere(back), slot, cleaned)
    return (lay_out(stokes), residual.reshape(blocks, det_local, sample_local))


def solution(mesh):
    placed = (
        P("tm", "det", None),
        P("tm", "det", None),
        P("tm", "det", None),
        P("tm", "det", None),
        P(),
    )
    return jax.shard_map(
        shards,
        mesh=mesh,
        in_specs=placed,
        out_specs=(P(None, ("tm", "det")), P("tm", "det", None)),
        check_vma=False,
    )
```

```python
import functools

import jax
import jax.numpy as jnp
from jax import lax
from jax.experimental import pallas as pl
from jax.experimental.pallas import tpu as pltpu
from jax.sharding import PartitionSpec as P

MODES = 16
NBINS = 1024
TILE_PIX = 32640
RIDGE = 1.0
LANES = 128
LO = 256
HI = -(-TILE_PIX // LO)
WIN = 32
HIP = HI + WIN - 8
SUB = 32
WAYS = LANES // SUB
GROUP = 8
PIX_BITS = 15
HALF = LANES // 2
F32 = jnp.float32
BF16 = jnp.bfloat16
HIGHEST = lax.Precision.HIGHEST
NT = (((1,), (1,)), ((), ()))
NN = (((1,), (0,)), ((), ()))
VMEM_LIMIT = 24 * 1024 * 1024
VMEM_SPEC = pl.BlockSpec(memory_space=pltpu.VMEM)


def iota(shape, dim):
    return lax.broadcasted_iota(jnp.int32, shape, dim)


def split3(x):
    first = x.astype(BF16).astype(F32)
    rest = x - first
    second = rest.astype(BF16).astype(F32)
    return first, second, rest - second


def split2(x):
    return split3(x)[:2]


def one_hot_cols(row, rows):
    ids = iota((rows, row.shape[1]), 0).astype(F32).astype(BF16)
    want = jnp.broadcast_to(row.astype(F32).astype(BF16), ids.shape)
    return jnp.where(ids == want, jnp.ones_like(ids), jnp.zeros_like(ids))


def modes_kernel(members, *refs):
    part_refs = refs[:-2]
    temp_ref, out_ref = refs[-2:]
    own_ref = part_refs[0]
    groups = own_ref.shape[0] // MODES
    templates = sum(ref[g * MODES : (g + 1) * MODES, :] for ref in part_refs for g in range(groups))
    templates = templates / members
    temp_ref[...] = templates
    both = jnp.concatenate([templates, own_ref[...]], axis=0)
    products = lax.dot_general(templates, both, NT, precision=HIGHEST, preferred_element_type=F32)
    pad = jnp.zeros((MODES, HALF - products.shape[1]), F32)
    half = jnp.concatenate([products, pad], axis=1)
    out_ref[...] = jnp.concatenate([half[: MODES // 2], half[MODES // 2 :]], axis=1)


def modes(parts, members):
    return pl.pallas_call(
        functools.partial(modes_kernel, members),
        out_shape=(
            jax.ShapeDtypeStruct((MODES, parts[0].shape[1]), F32),
            jax.ShapeDtypeStruct((MODES // 2, LANES), F32),
        ),
        in_specs=[VMEM_SPEC] * len(parts),
        out_specs=(VMEM_SPEC, VMEM_SPEC),
        compiler_params=pltpu.CompilerParams(vmem_limit_bytes=VMEM_LIMIT),
        name="modes",
    )(*parts)


def route_kernel(owner_ref, key_ref, load_ref, send_ref, idx_ref, keys, loads):
    tiles, rows = idx_ref.shape[0], idx_ref.shape[1]
    depth = key_ref.shape[0]
    keys[0:depth, :] = key_ref[...]
    loads[0:depth, :] = load_ref[...]
    keys[depth:, :] = jnp.zeros((8, LANES), jnp.int32)
    loads[depth:, :] = jnp.zeros((8, LANES), jnp.int32)
    sorted_keys = key_ref[...]
    lane = iota((8, LANES), 1)
    slot = iota((8, LANES), 0) * LANES + lane
    starts = [jnp.int32(0)]
    for tile in range(1, tiles):
        below = (sorted_keys < (tile << PIX_BITS)).astype(F32)
        starts.append(jnp.sum(below).astype(jnp.int32))
    starts.append(jnp.int32(depth * LANES))
    for tile in range(tiles):
        start = starts[tile]
        count = starts[tile + 1] - start
        top = start // LANES
        shift = start % LANES
        back = lax.rem(LANES - shift, LANES)
        whole = lane < LANES - shift

        def run(ref):
            turned = pltpu.roll(ref[pl.ds(top, 8), :], back, 1)
            return jnp.where(whole, turned, pltpu.roll(turned, 7, 0))

        key = run(keys)
        load = run(loads)
        live = slot < count
        owner = owner_ref[tile]
        pixel = jnp.where(live, key & ((1 << PIX_BITS) - 1), -1)
        index = jnp.where(live, load >> 10, -1)
        send_ref[owner, 0:rows, :] = pixel[0:rows]
        send_ref[owner, rows : 2 * rows, :] = (load & (NBINS - 1))[0:rows]
        idx_ref[owner, :, :] = index[0:rows]


def route(key, load, owner_map, owners, rows):
    flat = key.shape[0]
    depth = flat // LANES
    return pl.pallas_call(
        route_kernel,
        out_shape=(
            jax.ShapeDtypeStruct((owners, 2 * rows, LANES), jnp.int32),
            jax.ShapeDtypeStruct((owners, rows, LANES), jnp.int32),
        ),
        in_specs=[pl.BlockSpec(memory_space=pltpu.SMEM), VMEM_SPEC, VMEM_SPEC],
        out_specs=(VMEM_SPEC, VMEM_SPEC),
        scratch_shapes=[
            pltpu.VMEM((depth + 8, LANES), jnp.int32),
            pltpu.VMEM((depth + 8, LANES), jnp.int32),
        ],
        compiler_params=pltpu.CompilerParams(vmem_limit_bytes=VMEM_LIMIT),
        name="route",
    )(owner_map, key.reshape(depth, LANES), load.reshape(depth, LANES))


def sky_kernel(stokes_ref, sky_ref):
    for row in range(HI):
        first = row * LO
        width = min(LO, TILE_PIX - first)
        for q in range(3):
            sky_ref[q : q + 1, first : first + width] = stokes_ref[q, row : row + 1, :width]


def lay_out(stokes):
    return pl.pallas_call(
        sky_kernel,
        out_shape=jax.ShapeDtypeStruct((3, TILE_PIX), F32),
        in_specs=[VMEM_SPEC],
        out_specs=VMEM_SPEC,
        compiler_params=pltpu.CompilerParams(vmem_limit_bytes=VMEM_LIMIT),
        name="lay_out",
    )(stokes)


def pair_row(ref, pair, r):
    return jnp.concatenate([ref[2 * pair, r : r + 1, :], ref[2 * pair + 1, r : r + 1, :]], axis=1)


def pick_kernel(temp_ref, samples_ref, idx_ref, raw_ref, there_ref):
    det_local, length = samples_ref.shape
    owners, rows = idx_ref.shape[0], idx_ref.shape[1]
    terms = split3(samples_ref[...]) + split3(temp_ref[...])
    parts = jnp.concatenate(terms, axis=0).astype(BF16)
    det_id = iota((det_local, 2 * LANES), 0)

    def step(pair, _):
        for r in range(rows):
            index = pair_row(idx_ref, pair, r)
            found = lax.dot_general(
                parts, one_hot_cols(index & (length - 1), length), NN, preferred_element_type=F32
            )
            own = sum(found[i * det_local : (i + 1) * det_local] for i in range(3))
            here = jnp.where(det_id == index // length, own, 0.0)
            value = jnp.sum(here, axis=0, keepdims=True)
            raw_ref[2 * pair, r : r + 1, :] = value[:, :LANES]
            raw_ref[2 * pair + 1, r : r + 1, :] = value[:, LANES:]
            found = found[3 * det_local :]
            there_ref[pair, r] = sum(found[i * MODES : (i + 1) * MODES] for i in range(3))
        return 0

    lax.fori_loop(0, owners // 2, step, 0, unroll=16)


def pick(templates, samples, idx):
    owners, rows = idx.shape[:2]
    return pl.pallas_call(
        pick_kernel,
        out_shape=(
            jax.ShapeDtypeStruct(idx.shape, F32),
            jax.ShapeDtypeStruct((owners // 2, rows, MODES, 2 * LANES), F32),
        ),
        in_specs=[VMEM_SPEC] * 3,
        out_specs=(VMEM_SPEC, VMEM_SPEC),
        compiler_params=pltpu.CompilerParams(vmem_limit_bytes=VMEM_LIMIT),
        name="pick",
    )(templates, samples, idx)


def clean_kernel(length, raw_ref, there_ref, idx_ref, *refs):
    coef_ref, pay_ref = refs[-2:]
    det_local = coef_ref.shape[1]
    owners, rows = idx_ref.shape[0], idx_ref.shape[1]
    packed = sum(ref[...] for ref in refs[:-2])
    system = jnp.concatenate([packed, pltpu.roll(packed, HALF, 1)], axis=0)
    row_id = iota((MODES, LANES), 0)
    lane_id = iota((MODES, LANES), 1)
    system = system + jnp.where(row_id == lane_id, RIDGE, 0.0)
    for k in range(MODES):
        pivot = system[k : k + 1, :] / system[k : k + 1, k : k + 1]
        column = system[:, k : k + 1]
        system = jnp.where(row_id == k, pivot, system - column * pivot)
    coef = system[:, MODES : MODES + det_local]
    coef_ref[...] = coef
    parts = jnp.concatenate(split3(coef), axis=0).astype(BF16)

    def step(pair, _):
        for r in range(rows):
            index = pair_row(idx_ref, pair, r)
            found = lax.dot_general(
                parts,
                one_hot_cols(jnp.where(index < 0, det_local, index // length), det_local),
                NN,
                preferred_element_type=F32,
            )
            weight = sum(found[i * MODES : (i + 1) * MODES] for i in range(3))
            model = jnp.sum(weight * there_ref[pair, r], axis=0, keepdims=True)
            value = pair_row(raw_ref, pair, r) - model
            pay_ref[2 * pair, r : r + 1, :] = value[:, :LANES]
            pay_ref[2 * pair + 1, r : r + 1, :] = value[:, LANES:]
        return 0

    lax.fori_loop(0, owners // 2, step, 0, unroll=16)


def clean(sums, raw, there, idx, shape):
    det_local, length = shape
    return pl.pallas_call(
        functools.partial(clean_kernel, length),
        out_shape=(
            jax.ShapeDtypeStruct((MODES, det_local), F32),
            jax.ShapeDtypeStruct(idx.shape, F32),
        ),
        in_specs=[VMEM_SPEC] * (3 + len(sums)),
        out_specs=(VMEM_SPEC, VMEM_SPEC),
        compiler_params=pltpu.CompilerParams(vmem_limit_bytes=VMEM_LIMIT),
        name="clean",
    )(raw, there, idx, *sums)


def shuffle(blocks, lane):
    blocks = list(blocks)
    width = HALF
    while width >= SUB:
        low = (lane & width) == 0
        step = width // SUB
        for i in range(WAYS):
            if i & step == 0:
                a, b = blocks[i], blocks[i + step]
                blocks[i] = jnp.where(low, a, pltpu.roll(b, width, 1))
                blocks[i + step] = jnp.where(low, pltpu.roll(a, LANES - width, 1), b)
        width //= 2
    return blocks


def chunk_row(ref, run, group, r):
    return jnp.concatenate([ref[run, GROUP * group + i, r : r + 1, :] for i in range(GROUP)], axis=1)


def over_chunks(groups, rows, table_ref, body):
    def step(i, _):
        run, group = lax.rem(i, WAYS), lax.div(i, WAYS)
        ends = [(table_ref[r, 2 * i], table_ref[r, 2 * i + 1]) for r in range(rows)]
        widest = functools.reduce(jnp.maximum, [high - low for low, high in ends])

        for r in range(rows):
            body(run, group, r, ends[r][0], True)

        @pl.when(widest >= WIN // 8)
        def _():
            for r in range(rows):
                low, high = ends[r]

                def more(w, _):
                    body(run, group, r, low + w * (WIN // 8), False)
                    return 0

                lax.fori_loop(1, (high - low) // (WIN // 8) + 1, more, 0)

        return 0

    lax.fori_loop(0, groups * WAYS, step, 0, unroll=2)


def windows_of(pix_ref, groups, rows):
    table_lane = iota((rows, LANES), 1)
    windows = jnp.zeros((rows, LANES), jnp.int32)
    for group in range(groups):
        for run in range(WAYS):
            ends = [pix_ref[run, group * GROUP + i] for i in range(GROUP)]
            most = functools.reduce(jnp.maximum, ends)
            least = functools.reduce(
                jnp.minimum, [jnp.where(x < 0, TILE_PIX - 1, x) for x in ends]
            )
            most = jnp.max(most, axis=1, keepdims=True)
            least = jnp.min(least, axis=1, keepdims=True)
            high = most >> 11
            low = jnp.where(most < 0, 0, least >> 11)
            at = 2 * (group * WAYS + run)
            windows = jnp.where(table_lane == at, low, windows)
            windows = jnp.where(table_lane == at + 1, high, windows)
    return windows


def scatter_add(sum_ref, terms, pieces, pixel, first):
    start = pl.multiple_of(first * 8, 8)
    here = (iota((WIN, pixel.shape[1]), 0) + start) == (pixel >> 8)
    stacked = [jnp.where(here, jnp.broadcast_to(x, here.shape), 0.0) for x in pieces]
    found = lax.dot_general(
        jnp.concatenate(stacked, axis=0).astype(BF16),
        one_hot_cols(pixel & (LO - 1), LO),
        NT,
        preferred_element_type=F32,
    )
    at = 0
    for q, count in enumerate(terms):
        total = found[at : at + WIN]
        for i in range(1, count):
            total = total + found[at + i * WIN : at + (i + 1) * WIN]
        at += count * WIN
        sum_ref[q, pl.ds(start, WIN), :] += total


ANGLE_TERMS = (1, 3, 3, 3, 3)
VALUE_TERMS = (2, 3, 3)


def angles_kernel(got_ref, mixed_ref, sum_ref, pix_ref, parts_ref, table_vmem, table, sem):
    owners, rows = got_ref.shape[0], mixed_ref.shape[3]
    groups = owners // WAYS // GROUP
    lane = iota((2 * rows, LANES), 1)
    for at in range(owners // WAYS):
        mixed = shuffle([got_ref[at * WAYS + i] for i in range(WAYS)], lane)
        for run in range(WAYS):
            pix_ref[run, at] = mixed[run][:rows]
            mixed_ref[0, run, at] = mixed[run][:rows].astype(F32)
    table_vmem[...] = windows_of(pix_ref, groups, rows)
    copy = pltpu.make_async_copy(table_vmem, table, sem)
    copy.start()
    for at in range(owners // WAYS):
        mixed = shuffle([got_ref[at * WAYS + i] for i in range(WAYS)], lane)
        for run in range(WAYS):
            angle = (jnp.pi * mixed[run][rows:].astype(F32) / NBINS) * 2.0
            cosine, sine = jnp.cos(angle), jnp.sin(angle)
            mixed_ref[1, run, at] = cosine
            mixed_ref[2, run, at] = sine
            parts = (
                split3(cosine) + split3(sine) + split3(cosine * cosine) + split3(cosine * sine)
            )
            for p, part in enumerate(parts):
                parts_ref[p, run, at] = part
    sum_ref[...] = jnp.zeros_like(sum_ref)
    copy.wait()

    def add(run, group, r, first, _):
        pixel = chunk_row(pix_ref, run, group, r)
        pieces = [jnp.ones(pixel.shape, F32)]
        pieces += [chunk_row(parts_ref.at[p], run, group, r) for p in range(parts_ref.shape[0])]
        scatter_add(sum_ref, ANGLE_TERMS, pieces, pixel, first)

    over_chunks(groups, rows, table, add)


def angles(got, rows):
    mixed = (WAYS, got.shape[0] // WAYS, rows, LANES)
    return pl.pallas_call(
        angles_kernel,
        out_shape=(
            jax.ShapeDtypeStruct((3,) + mixed, F32),
            jax.ShapeDtypeStruct((len(ANGLE_TERMS), HIP, LO), F32),
        ),
        in_specs=[VMEM_SPEC],
        out_specs=(VMEM_SPEC, VMEM_SPEC),
        scratch_shapes=[
            pltpu.VMEM(mixed, jnp.int32),
            pltpu.VMEM((sum(ANGLE_TERMS) - 1,) + mixed, F32),
            pltpu.VMEM((rows, LANES), jnp.int32),
            pltpu.SMEM((rows, LANES), jnp.int32),
            pltpu.SemaphoreType.DMA,
        ],
        compiler_params=pltpu.CompilerParams(vmem_limit_bytes=VMEM_LIMIT),
        name="angles",
    )(got)


def solve_stokes(sums):
    a11 = sums[0] + RIDGE
    a12 = sums[1]
    a13 = sums[2]
    a22 = sums[3] + RIDGE
    a23 = sums[4]
    a33 = sums[5] + RIDGE
    c11 = a22 * a33 - a23 * a23
    c12 = a13 * a23 - a12 * a33
    c13 = a12 * a23 - a13 * a22
    c22 = a11 * a33 - a13 * a13
    c23 = a12 * a13 - a11 * a23
    c33 = a11 * a22 - a12 * a12
    inverse = 1.0 / (a11 * c11 + a12 * c12 + a13 * c13)
    stokes_i = (c11 * sums[6] + c12 * sums[7] + c13 * sums[8]) * inverse
    stokes_q = (c12 * sums[6] + c22 * sums[7] + c23 * sums[8]) * inverse
    stokes_u = (c13 * sums[6] + c23 * sums[7] + c33 * sums[8]) * inverse
    return (stokes_i, stokes_q, stokes_u)


def map_kernel(
    got_ref, mixed_ref, acc_ref, sum_ref, back_ref, pix_ref, parts_ref, table_vmem, table, sem
):
    owners, rows = got_ref.shape[0], got_ref.shape[1]
    groups = owners // WAYS // GROUP
    lane = iota((rows, LANES), 1)
    cos_ref, sin_ref = mixed_ref.at[1], mixed_ref.at[2]
    pix_ref[...] = mixed_ref[0].astype(jnp.int32)
    table_vmem[...] = windows_of(pix_ref, groups, rows)
    copy = pltpu.make_async_copy(table_vmem, table, sem)
    copy.start()
    for at in range(owners // WAYS):
        mixed = shuffle([got_ref[at * WAYS + i] for i in range(WAYS)], lane)
        for run in range(WAYS):
            value, cosine, sine = mixed[run], cos_ref[run, at], sin_ref[run, at]
            parts = split2(value) + split3(cosine * value) + split3(sine * value)
            for p, part in enumerate(parts):
                parts_ref[p, run, at] = part
    sum_ref[...] = jnp.zeros_like(sum_ref)
    copy.wait()

    def add(run, group, r, first, _):
        pixel = chunk_row(pix_ref, run, group, r)
        pieces = [chunk_row(parts_ref.at[p], run, group, r) for p in range(parts_ref.shape[0])]
        scatter_add(sum_ref, VALUE_TERMS, pieces, pixel, first)

    over_chunks(groups, rows, table, add)

    for block in range(HI // 8):
        at = pl.ds(block * 8, 8)
        sums = [acc_ref[q, at, :] for q in range(5)]
        sums += [sums[0] - sums[3]] + [sum_ref[q, at, :] for q in range(3)]
        stokes = solve_stokes(sums)
        for q in range(3):
            sum_ref[q, at, :] = stokes[q]

    def look(run, group, r, first, fresh):
        pixel = chunk_row(pix_ref, run, group, r)
        start = pl.multiple_of(first * 8, 8)
        planes = [x for q in range(3) for x in split2(sum_ref[q, pl.ds(start, WIN), :])]
        found = lax.dot_general(
            jnp.concatenate(planes, axis=0).astype(BF16),
            one_hot_cols(pixel & (LO - 1), LO),
            NN,
            preferred_element_type=F32,
        )
        stokes = [
            found[2 * q * WIN : (2 * q + 1) * WIN] + found[(2 * q + 1) * WIN : (2 * q + 2) * WIN]
            for q in range(3)
        ]
        cosine = chunk_row(cos_ref, run, group, r)
        sine = chunk_row(sin_ref, run, group, r)
        signal = stokes[0] + cosine * stokes[1] + sine * stokes[2]
        here = (iota(signal.shape, 0) + start) == (pixel >> 8)
        value = jnp.sum(jnp.where(here, signal, 0.0), axis=0, keepdims=True)
        for i in range(GROUP):
            part = value[:, i * LANES : (i + 1) * LANES]
            if fresh:
                parts_ref[0, run, GROUP * group + i, r : r + 1, :] = part
            else:
                parts_ref[0, run, GROUP * group + i, r : r + 1, :] += part

    over_chunks(groups, rows, table, look)

    for at in range(owners // WAYS):
        mixed = shuffle([parts_ref[0, run, at] for run in range(WAYS)], lane)
        for i in range(WAYS):
            back_ref[at * WAYS + i] = mixed[i]


def make_map(got, mixed, acc):
    rows = got.shape[1]
    return pl.pallas_call(
        map_kernel,
        out_shape=(
            jax.ShapeDtypeStruct((3, HIP, LO), F32),
            jax.ShapeDtypeStruct(got.shape, F32),
        ),
        in_specs=[VMEM_SPEC] * 3,
        out_specs=(VMEM_SPEC, VMEM_SPEC),
        scratch_shapes=[
            pltpu.VMEM(mixed.shape[1:], jnp.int32),
            pltpu.VMEM((sum(VALUE_TERMS),) + mixed.shape[1:], F32),
            pltpu.VMEM((rows, LANES), jnp.int32),
            pltpu.SMEM((rows, LANES), jnp.int32),
            pltpu.SemaphoreType.DMA,
        ],
        compiler_params=pltpu.CompilerParams(vmem_limit_bytes=VMEM_LIMIT),
        name="make_map",
    )(got, mixed, acc)


def invert_kernel(idx_ref, coef_ref, temp_ref, samples_ref, slot_ref, clean_ref):
    det_local, length = slot_ref.shape
    clean_ref[...] = samples_ref[...] - lax.dot_general(
        coef_ref[...],
        temp_ref[...],
        (((0,), (0,)), ((), ())),
        precision=HIGHEST,
        preferred_element_type=F32,
    )
    owners, rows = idx_ref.shape[0], idx_ref.shape[1]
    det_id = iota((det_local, 2 * LANES), 0)
    lane = lax.rem(iota((1, 2 * LANES), 1), LANES).astype(F32)
    second = (iota((1, 2 * LANES), 1) >= LANES).astype(jnp.int32)

    def step(pair, total):
        for r in range(rows):
            index = jnp.concatenate(
                [idx_ref[2 * pair, r : r + 1, :], idx_ref[2 * pair + 1, r : r + 1, :]], axis=1
            )
            row = ((2 * pair + second) * rows + r).astype(F32)
            here = det_id == index // length
            stacked = [
                jnp.where(here, jnp.broadcast_to(piece, here.shape), 0.0) for piece in (row, lane)
            ]
            total = total + lax.dot_general(
                jnp.concatenate(stacked, axis=0).astype(BF16),
                one_hot_cols(index & (length - 1), length),
                NT,
                preferred_element_type=F32,
            )
        return total

    total = lax.fori_loop(
        0, owners // 2, step, jnp.zeros((2 * det_local, length), F32), unroll=16
    )
    slot_ref[...] = (total[:det_local] * LANES + total[det_local:]).astype(jnp.int32)


def invert(idx, coef, templates, samples):
    return pl.pallas_call(
        invert_kernel,
        out_shape=(
            jax.ShapeDtypeStruct(samples.shape, jnp.int32),
            jax.ShapeDtypeStruct(samples.shape, F32),
        ),
        in_specs=[VMEM_SPEC] * 4,
        out_specs=(VMEM_SPEC, VMEM_SPEC),
        compiler_params=pltpu.CompilerParams(vmem_limit_bytes=VMEM_LIMIT),
        name="invert",
    )(idx, coef, templates, samples)


def residual_kernel(got_ref, slot_ref, clean_ref, out_ref, rows_ref):
    owners, rows = got_ref.shape[0], got_ref.shape[1]
    for o in range(owners):
        rows_ref[o * rows : (o + 1) * rows, :] = got_ref[o]
    parts = jnp.concatenate(split2(rows_ref[...]), axis=0).astype(BF16)
    depth = owners * rows
    row_id = iota((depth, slot_ref.shape[1]), 0)
    for d in range(slot_ref.shape[0]):
        slot = slot_ref[d : d + 1, :]
        found = lax.dot_general(
            parts, one_hot_cols(slot & (LANES - 1), LANES), NN, preferred_element_type=F32
        )
        here = jnp.where(row_id == slot >> 7, found[:depth] + found[depth:], 0.0)
        out_ref[d : d + 1, :] = clean_ref[d : d + 1, :] - jnp.sum(here, axis=0, keepdims=True)


def residuals(got, slot, cleaned):
    return pl.pallas_call(
        residual_kernel,
        out_shape=jax.ShapeDtypeStruct(cleaned.shape, F32),
        in_specs=[VMEM_SPEC] * 3,
        out_specs=VMEM_SPEC,
        scratch_shapes=[pltpu.VMEM((got.shape[0] * got.shape[1], LANES), F32)],
        compiler_params=pltpu.CompilerParams(vmem_limit_bytes=VMEM_LIMIT),
        name="residuals",
    )(got, slot, cleaned)


def shards(timestream, tile_index, pixel_index, angle_bin, owner_map):
    blocks, det_local, sample_local = timestream.shape
    samples = timestream[0]
    tm_count = lax.axis_size("tm")
    det_count = lax.axis_size("det")
    owners = tm_count * det_count
    flat = det_local * sample_local
    rows = flat // (owners // 2) // LANES

    parts = [samples] + [
        lax.ppermute(samples, "det", [(i, (i + k) % det_count) for i in range(det_count)])
        for k in range(1, det_count)
    ]
    def flatten(x):
        x = x.reshape(det_local // 8, 8, sample_local // LANES, LANES)
        return x.transpose(0, 2, 1, 3).reshape(flat)

    number = jnp.arange(flat, dtype=jnp.int32).reshape(tile_index.shape)
    key = flatten((tile_index << PIX_BITS) + pixel_index)
    load = flatten((number << 10) + angle_bin)
    templates, products = modes(parts, det_local * det_count // MODES)

    def partners(x, bit):
        return lax.ppermute(x, "tm", [(i, i ^ bit) for i in range(tm_count)])

    bits = [1 << i for i in reversed(range(tm_count.bit_length() - 1))]
    key, load, products = lax.optimization_barrier((key, load, products))
    found = partners(products, bits[0])
    key, load = lax.sort((key, load), num_keys=1, is_stable=False)
    key, load, found = lax.optimization_barrier((key, load, found))
    products = products + found
    found = partners(products, bits[1])
    send, idx = route(key, load, owner_map, owners, rows)
    send, found = lax.optimization_barrier((send, found))
    for bit in bits[2:]:
        products = products + found
        found = partners(products, bit)
    products = [products, found]
    everywhere = functools.partial(
        lax.all_to_all, axis_name=("tm", "det"), split_axis=0, concat_axis=0, tiled=True
    )
    got = everywhere(send)
    raw, there = pick(templates, samples, idx)
    coef, pay = clean(products, raw, there, idx, samples.shape)
    mixed, acc = angles(got, rows)

    values = everywhere(pay)
    stokes, back = make_map(values, mixed, acc)
    slot, cleaned = invert(idx, coef, templates, samples)
    residual = residuals(everywhere(back), slot, cleaned)
    return (lay_out(stokes), residual.reshape(blocks, det_local, sample_local))


def solution(mesh):
    placed = (
        P("tm", "det", None),
        P("tm", "det", None),
        P("tm", "det", None),
        P("tm", "det", None),
        P(),
    )
    return jax.shard_map(
        shards,
        mesh=mesh,
        in_specs=placed,
        out_specs=(P(None, ("tm", "det")), P("tm", "det", None)),
        check_vma=False,
    )
```
